32 devices in a mesh: node: 8 (over z, y), rep: 4 (over x, core).
Axes of the slice: x: 2, y: 2, z: 4, core: 2. Of those that a mesh axis runs over, the one named last changes fastest.
Arguments:
- features: bfloat16 [16384, 256], P('node'), may hold values from -6 to 6
- tiles: bfloat16 [8, 4, 4, 96, 128, 128], P('node', 'rep'), may hold values from -0.09375 to 0.09375
- tile_rows: int32 [8, 4, 4, 96], P('node', 'rep'), may hold values from 0 to 15
- tile_cols: int32 [8, 4, 4, 96], P('node', 'rep'), may hold values from 0 to 15
- tile_count: int32 [8, 4, 4], P('node', 'rep'), may hold values from 1 to 96, as said below
- order: int32 [16384], P('node'), may hold values from 0 to 16383, as said below
- weight: bfloat16 [256, 256], replicated, may hold values from -0.375 to 0.375
- cotangent: bfloat16 [16384, 256], P(('node', 'rep')), may hold values from -6 to 6
Outputs:
- activated: bfloat16 [16384, 256], P(('node', 'rep'))
- feature_grad: bfloat16 [16384, 256], P(('node', 'rep'))
- weight_grad: float32 [256, 256], replicated
The draws below stay inside these ranges and needn't reach their ends.
Inputs may be any that keep to these rules, and one draw needn't show every extreme that they name: `tile_count`: for every node block and offset, exactly one tile group holds 96 live slots; the counts of the others lie between 1 and 32. order is a permutation of the nodes that maps each aligned block of 512 positions onto itself.
All inputs are finite; a program needn't handle non-finite values.
Results may differ from the reference program's by a relative error of at most 0.017.
Values may be sent and summed in bfloat16 or wider, within the bound.
A program may use at most 128 MiB of HBM per device.

```python
import math
import jax
import jax.numpy as jnp
from jax import lax

F = 256
TILE = 128
CAPK = 96
BLOCKS = 8
REPS = 4
RB = 16
QROWS = 512
NODES = 16384


def draw_tile_count(key, part):
    first_key = jax.random.fold_in(key, 11)
    second_key = jax.random.fold_in(key, 23)
    base_count = jax.random.randint(first_key, (BLOCKS, REPS, 4), 1, max(2, CAPK // 3 + 1))
    busy_rep = jax.random.randint(second_key, (BLOCKS, 1, 4), 0, REPS)
    rep_ids = jnp.arange(REPS, dtype=jnp.int32)[None, :, None]
    return jnp.where(rep_ids == busy_rep, CAPK, base_count).astype(jnp.int32)


def draw_order(key, part):
    first_key = jax.random.fold_in(key, 37)
    block_count = NODES // QROWS
    scores = jax.random.randint(first_key, (block_count, QROWS), 0, 2 ** 30)
    within = jnp.argsort(scores, axis=1).astype(jnp.int32)
    starts = (jnp.arange(block_count, dtype=jnp.int32) * QROWS)[:, None]
    return (within + starts).reshape(NODES).astype(jnp.int32)


def touch_ends(entries, key, smallest, largest):
    spot = [jax.random.randint(jax.random.fold_in(key, axis), (), 0, length) for axis, length in enumerate(entries.shape)]
    widest = entries.shape.index(max(entries.shape))
    neighbour = spot[:widest] + [(spot[widest] + 1) % entries.shape[widest]] + spot[widest + 1:]
    return entries.at[tuple(spot)].set(smallest).at[tuple(neighbour)].set(largest)


def levels(key, extent, split, low, high):
    def one(dim, shards_of):
        draws = jax.random.uniform(jax.random.fold_in(jax.random.fold_in(key, 6), dim), (shards_of,), jnp.float32, low / len(split), high / len(split))
        return jnp.repeat(jnp.exp(draws), extent[dim] // shards_of).reshape((-1,) + (1,) * (len(extent) - dim - 1))

    factor_of = one(*split[0])
    for cut in split[1:]:
        factor_of = factor_of * one(*cut)
    return factor_of


def scatter_about(rng, shape, scale, bound, shards=(), kind=jnp.bfloat16):
    result = jax.random.normal(rng, shape, jnp.float32) * scale
    if len(shards) > 0:
        result = levels(rng, shape, shards, -0.22, 0.18) * result
    return jnp.clip(result, min=-bound, max=bound).astype(kind)


def setup_inputs(seed: int = 0) -> dict:
    seeds = jax.random.split(jax.random.key(seed), 9)
    features = scatter_about(seeds[0], (NODES, F), 1.0, 6.0, ((0, 8),))
    tiles = scatter_about(seeds[1], (BLOCKS, REPS, 4, CAPK, TILE, TILE), (6 * CAPK * TILE // RB) ** -0.5, 0.09375, ((0, 8), (1, 4)))
    tile_rows = touch_ends(jax.random.randint(seeds[2], (BLOCKS, REPS, 4, CAPK), 0, RB), jax.random.fold_in(seeds[2], 1), 0, RB - 1).astype(jnp.int32)
    tile_cols = touch_ends(jax.random.randint(seeds[3], (BLOCKS, REPS, 4, CAPK), 0, RB), jax.random.fold_in(seeds[3], 1), 0, RB - 1).astype(jnp.int32)
    tile_count = draw_tile_count(jax.random.fold_in(seeds[8], 71), 0)
    order = draw_order(jax.random.fold_in(seeds[8], 71), 0)
    weight = scatter_about(seeds[6], (F, F), F ** -0.5, 0.375)
    cotangent = scatter_about(seeds[7], (NODES, F), 1.0, 6.0, ((0, 32),))
    return {"features": features, "tiles": tiles, "tile_rows": tile_rows, "tile_cols": tile_cols, "tile_count": tile_count, "order": order, "weight": weight, "cotangent": cotangent}


def reference(features, tiles, tile_rows, tile_cols, tile_count, order, weight, cotangent):
    feat_width = features.shape[1]
    reordered = features[order]
    blocks = reordered.reshape(BLOCKS, RB, TILE, feat_width)
    slot_ids = jnp.arange(CAPK, dtype=jnp.int32)

    def masked(block_id, offset):
        live_mask = (slot_ids[None, :] < tile_count[block_id, :, offset][:, None]).astype(jnp.float32)
        return tiles[block_id, :, offset].astype(jnp.float32) * live_mask[:, :, None, None]

    def forward_block(block_id):
        totals = jnp.zeros((RB, TILE, feat_width), jnp.float32)
        for offset in range(4):
            source = blocks[(block_id + 1 - offset) % BLOCKS]
            gathered = source[tile_cols[block_id, :, offset]].astype(jnp.float32)
            products = jnp.einsum('rcab,rcbf->rcaf', masked(block_id, offset), gathered)
            totals = totals.at[tile_rows[block_id, :, offset].reshape(-1)].add(products.reshape(-1, TILE, feat_width))
        return totals
    aggregate = lax.map(forward_block, jnp.arange(BLOCKS, dtype=jnp.int32)).reshape(NODES, feat_width).astype(jnp.bfloat16)
    pre_act = jnp.dot(aggregate, weight, preferred_element_type=jnp.float32)
    gate_val = jax.nn.sigmoid(pre_act)
    activated = (pre_act * gate_val).astype(jnp.bfloat16)
    pre_grad = (cotangent.astype(jnp.float32) * gate_val * (1.0 + pre_act * (1.0 - gate_val))).astype(jnp.bfloat16)
    weight_grad = jnp.dot(aggregate.T, pre_grad, preferred_element_type=jnp.float32) * (1.0 / math.sqrt(NODES))
    back_rows = jnp.dot(pre_grad, weight.T, preferred_element_type=jnp.float32).astype(jnp.bfloat16)
    back_blocks = back_rows.reshape(BLOCKS, RB, TILE, feat_width)

    def backward_block(block_id):
        totals = jnp.zeros((RB, TILE, feat_width), jnp.float32)
        for offset in range(4):
            owner = (block_id - 1 + offset) % BLOCKS
            gathered = back_blocks[owner][tile_rows[owner, :, offset]].astype(jnp.float32)
            products = jnp.einsum('rcab,rcaf->rcbf', masked(owner, offset), gathered)
            totals = totals.at[tile_cols[owner, :, offset].reshape(-1)].add(products.reshape(-1, TILE, feat_width))
        return totals
    reordered_grad = lax.map(backward_block, jnp.arange(BLOCKS, dtype=jnp.int32)).reshape(NODES, feat_width)
    feature_grad = jnp.zeros((NODES, feat_width), jnp.float32).at[order].set(reordered_grad).astype(jnp.bfloat16)
    return (activated, feature_grad, weight_grad)
```

```python
import functools
import math

import jax
import jax.numpy as jnp
from jax import lax
from jax.experimental import pallas as pl
from jax.experimental.pallas import tpu as pltpu
from jax.sharding import PartitionSpec as P

EXCL = 3
SHARED = 2
EARLY = 3
GROUP = 14
FIELDS = 4
F32 = jnp.float32
BF16 = jnp.bfloat16


def table_kernel(capacity, count_ref, rows, cols, out, stage):
    lanes = stage.shape[1]
    stage[...] = jnp.zeros_like(stage)
    stage[0:4, 0:capacity] = rows[...].astype(F32)
    stage[4:8, 0:capacity] = cols[...].astype(F32)
    by_slot = stage[...].T
    sub = lax.broadcasted_iota(jnp.int32, (lanes, lanes), 0)
    lane = lax.broadcasted_iota(jnp.int32, (lanes, lanes), 1)
    lane_f = lane.astype(F32)
    before = (lane < sub).astype(BF16)
    upper = (sub < lane).astype(BF16)
    head = lax.broadcasted_iota(jnp.int32, (8, lanes), 0)
    for way in range(2):
        for k in range(4):
            key = by_slot[:, way * 4 + k : way * 4 + k + 1]
            live = sub < count_ref[k]
            mine = jnp.where(live & (key == lane_f), 1.0, 0.0)
            ahead = jnp.dot(before, mine.astype(BF16), preferred_element_type=F32)
            held = jnp.sum(mine, axis=0, keepdims=True)
            pairs = jnp.floor((held + 1.0) * 0.5)
            base = jnp.dot(
                jnp.broadcast_to(pairs, (8, lanes)).astype(BF16), upper, preferred_element_type=F32
            )[0:1]
            rank = jnp.sum(mine * ahead, axis=1, keepdims=True)
            spot = jnp.sum(mine * (2.0 * base), axis=1, keepdims=True) + rank
            put = jnp.where(live & (spot == lane_f), 1.0, 0.0)
            starts = jnp.sum(jnp.where(rank == 0.0, put, 0.0), axis=0, keepdims=True)
            other = stage[(1 - way) * 4 + k : (1 - way) * 4 + k + 1, :]
            values = jnp.where(
                head == 0, lane_f[0:8], jnp.where(head == 1, jnp.broadcast_to(other, (8, lanes)), 1.0)
            )
            found = jnp.dot(values.astype(BF16), put.astype(BF16), preferred_element_type=F32)
            slot = jnp.where(found[2:3] > 0.0, found[0:1], float(capacity))
            last = jnp.where(held > 0.0, base + pairs, 0.0)
            at = (way * 4 + k) * FIELDS
            out[at : at + 1, :] = slot.astype(jnp.int32)
            out[at + 1 : at + 2, :] = found[1:2].astype(jnp.int32)
            out[at + 2 : at + 3, :] = (1.0 - starts).astype(jnp.int32)
            out[at + 3 : at + 4, :] = last.astype(jnp.int32)


def table_call(count, rows, cols):
    capacity = rows.shape[-1]
    vmem = pl.BlockSpec(memory_space=pltpu.VMEM)
    return pl.pallas_call(
        functools.partial(table_kernel, capacity),
        out_shape=jax.ShapeDtypeStruct((8 * FIELDS, 128), jnp.int32),
        in_specs=[pl.BlockSpec(memory_space=pltpu.SMEM), vmem, vmem],
        out_specs=vmem,
        scratch_shapes=[pltpu.VMEM((128, 128), F32)],
        compiler_params=pltpu.CompilerParams(vmem_limit_bytes=4 * 1024 * 1024),
    )(count, rows, cols)


class Wires:
    def __init__(self, send, recv):
        self.send, self.recv, self.used = send, recv, 0

    def copy(self, src, dst, axis, target):
        at = self.used
        self.used += 1
        return pltpu.make_async_remote_copy(
            src_ref=src,
            dst_ref=dst,
            send_sem=self.send.at[at],
            recv_sem=self.recv.at[at],
            device_id={axis: target},
            device_id_type=pl.DeviceIdType.MESH,
        )

    def hop(self, src, dst, axis, target):
        copy = self.copy(src, dst, axis, target)
        copy.start()
        return copy


def fused_kernel(
    nodes, scale, table, tiles, features, order, cot, weight, act, grad, wgrad,
    held, here, halo_a, halo_b, halo_c, sums, acc, part, near, outgoing, far, agg, pg, full,
    terms, tnear, tout, tfar, leaving, got, lleave, lgot, total, lout, lfar,
    wmine, wnear, wout, wfar, wstep, wgot, wfull, pick,
    load_sems, send, recv,
):
    capacity = tiles.shape[1]
    count, size, feat = here.shape
    tq = count // 4
    quarter = tq * size
    pairs = (capacity + count) // 2
    me, home = lax.axis_index("rep"), lax.axis_index("node")
    x, c = me // 2, me % 2
    sib, across, diag = x * 2 + 1 - c, (1 - x) * 2 + c, (1 - x) * 2 + 1 - c
    wires = Wires(send, recv)

    def to_node(d):
        return (home + d) % nodes

    doubling = [1 << i for i in range(nodes.bit_length() - 1)]
    partners = []
    for step in doubling:
        low = (home // step) % 2
        partners.append(home + step - 2 * step * low)
    peers = [("rep", sib), ("rep", across)]
    peers += [("node", to_node(d)) for d in (1, nodes - 1, 2, nodes - 2)]
    peers += [("node", p) for p in partners]
    barrier = pltpu.get_barrier_semaphore()
    for axis, target in peers:
        pl.semaphore_signal(
            barrier, inc=1, device_id={axis: target}, device_id_type=pl.DeviceIdType.MESH
        )

    loads = [
        pltpu.make_async_copy(
            tiles.at[k], held.at[k, pl.ds(0, capacity)], load_sems.at[k]
        )
        for k in (1, 0, 2, 3)
    ]
    for load in loads:
        load.start()

    spots = lax.broadcasted_iota(jnp.int32, (quarter, size), 0)

    def chosen(t):
        return (spots == lax.rem(order[pl.ds(t, 1), :], quarter)).astype(BF16)

    def reorder(t):
        rows = features[pl.ds(pl.multiple_of((t // tq) * quarter, quarter), quarter), :]
        here[t] = lax.dot_general(
            chosen(t), rows, (((0,), (0,)), ((), ())), preferred_element_type=F32
        ).astype(BF16)

    first = 10 * x + EXCL * c
    common = 2 * 2 * EXCL // 2 + SHARED * c
    other = 10 * (1 - x) + EXCL * c
    for i in range(EXCL):
        reorder(first + i)
    for i in range(SHARED):
        reorder(common + i)
    pl.semaphore_wait(barrier, len(peers))

    moves = ((nodes - 1, halo_a), (1, halo_b), (2, halo_c))
    direct, shared = [], []
    for d, land in moves:
        direct.append(
            [
                wires.hop(here.at[first + i], land.at[first + i], "node", to_node(d))
                for i in range(EXCL)
            ]
        )
        block = pl.ds(common, SHARED)
        shared.append(wires.hop(here.at[block], land.at[block], "node", to_node(d)))
    for i in range(EXCL):
        reorder(other + i)
    rest = 10 * x + EXCL * (1 - c)
    for i in range(EXCL):
        reorder(rest + i)
        reorder(10 * (1 - x) + EXCL * (1 - c) + i)
    for i in range(SHARED):
        reorder(2 * EXCL + SHARED * (1 - c) + i)
    for k in range(4):
        held[k, capacity] = jnp.zeros((size, size), BF16)
    sums[0] = jnp.zeros((size, feat), F32)
    mine_pick = jnp.concatenate([chosen(me * tq + i) for i in range(tq)], axis=1)
    pick[...] = mine_pick

    crossing, aside_direct, aside_cross, aside_shared = [], [], [], []
    for d, land in moves:
        for i in range(EXCL):
            near_tile, far_tile = land.at[first + i], land.at[other + i]
            crossing.append(wires.copy(near_tile, near_tile, "rep", across))
            aside_direct.append(wires.copy(near_tile, near_tile, "rep", sib))
            aside_cross.append(wires.copy(far_tile, far_tile, "rep", sib))
        both = land.at[pl.ds(common, SHARED)]
        aside_shared.append(wires.copy(both, both, "rep", sib))

    def event_direct(g):
        direct[g // EXCL][g % EXCL].wait()
        crossing[g].start()
        aside_direct[g].start()

    def event_cross(g):
        crossing[g].wait()
        aside_cross[g].start()

    def event_shared(j):
        shared[j].wait()
        aside_shared[j].start()

    def settle(j):
        for i in range(EXCL):
            aside_direct[j * EXCL + i].wait()
            aside_cross[j * EXCL + i].wait()
        aside_shared[j].wait()

    def product(way, k, i, source):
        at = (way * 4 + k) * FIELDS
        one, two = held[k, table[at, 2 * i]], held[k, table[at, 2 * i + 1]]
        left, right = source[table[at + 1, 2 * i]], source[table[at + 1, 2 * i + 1]]
        rows = jnp.concatenate([left, right], axis=0)
        if way == 0:
            return jnp.dot(
                jnp.concatenate([one, two], axis=1), rows, preferred_element_type=F32
            )
        return lax.dot_general(
            jnp.concatenate([one, two], axis=0), rows, (((0,), (0,)), ((), ())),
            preferred_element_type=F32,
        )

    def sweep(way, k, source, events):
        at = (way * 4 + k) * FIELDS

        def body(step, _):
            for turn, work in enumerate(events):
                if work:
                    @pl.when(step == turn)
                    def _(work=work):
                        for f in work:
                            f()
            base = step * GROUP
            products = [product(way, k, base + g, source) for g in range(GROUP)]
            value = sums[base]
            for g in range(GROUP):
                value = products[g] + table[at + 2, 2 * (base + g)].astype(F32) * value
                sums[base + g + 1] = value
            return 0

        lax.fori_loop(0, pairs // GROUP, body, 0)

    def ends(way, k, r):
        return sums[table[(way * 4 + k) * FIELDS + 3, r]]

    def run(*work):
        for f in work:
            f()

    E = lambda g: (lambda: event_direct(g))
    X = lambda g: (lambda: event_cross(g))
    S = lambda j: (lambda: event_shared(j))

    for load in loads:
        load.wait()
    sweep(0, 1, here, [[E(0)], [E(1)], [E(2), X(0)], [E(3), X(1)]])
    for r in range(count):
        acc[r] = ends(0, 1, r)
    run(E(4), X(2), S(0))
    settle(0)
    sweep(0, 0, halo_a, [[E(5), X(3)], [E(6), X(4)], [E(7), X(5)], [E(8), X(6)]])
    for r in range(count):
        acc[r] += ends(0, 0, r)
    run(S(1))
    settle(1)
    sweep(0, 2, halo_b, [[X(7)], [X(8), S(2)], [], []])
    for r in range(count):
        acc[r] += ends(0, 2, r)
    settle(2)
    sweep(0, 3, halo_c, [[], [], [], []])

    def finish_rows(q):
        for i in range(tq):
            r = q * tq + i
            value = acc[r] + ends(0, 3, r)
            acc[r] = value
            part[r] = value.astype(BF16)

    finish_rows(diag)
    to_sib = [
        wires.hop(part.at[diag * tq + i], near.at[i], "rep", sib) for i in range(tq)
    ]
    finish_rows(sib)
    block = pl.ds(sib * tq, tq)
    rest_sib = wires.hop(part.at[block], near.at[pl.ds(tq, tq)], "rep", sib)
    finish_rows(across)
    crossed = []
    for i in range(tq):
        to_sib[i].wait()
        outgoing[i] = (acc[across * tq + i] + near[i].astype(F32)).astype(BF16)
        crossed.append(wires.hop(outgoing.at[i], far.at[i], "rep", across))
    finish_rows(me)
    rest_sib.wait()
    over, side, relay = [], [], []
    for i in range(tq):
        r = me * tq + i
        mine = acc[r] + near[tq + i].astype(F32)
        crossed[i].wait()
        aggregate = (mine + far[i].astype(F32)).astype(BF16)
        agg[i * size : (i + 1) * size, :] = aggregate
        pre_act = jnp.dot(aggregate, weight[...], preferred_element_type=F32)
        gate = jax.nn.sigmoid(pre_act)
        act[i * size : (i + 1) * size, :] = (pre_act * gate).astype(act.dtype)
        pre_grad = (
            cot[i * size : (i + 1) * size, :].astype(F32) * gate * (1.0 + pre_act * (1.0 - gate))
        ).astype(BF16)
        pg[i * size : (i + 1) * size, :] = pre_grad
        full[r] = lax.dot_general(
            pre_grad, weight[...], (((1,), (1,)), ((), ())), preferred_element_type=F32
        ).astype(BF16)
        over.append(wires.hop(full.at[r], full.at[r], "rep", across))
        side.append(wires.hop(full.at[r], full.at[r], "rep", sib))
    wrows = feat // 4
    wpart = lax.dot_general(
        agg[...], pg[...], (((0,), (0,)), ((), ())), preferred_element_type=F32
    )
    for q in range(4):
        wmine[q] = wpart[q * wrows : (q + 1) * wrows, :].astype(BF16)
    for i in range(tq):
        over[i].wait()
        r = across * tq + i
        relay.append(wires.hop(full.at[r], full.at[r], "rep", sib))
    wsib = [
        wires.hop(wmine.at[diag], wnear.at[0], "rep", sib),
        wires.hop(wmine.at[sib], wnear.at[1], "rep", sib),
    ]
    for copy in side + relay:
        copy.wait()

    late = tq - EARLY
    flight = {}
    for k, j, d in ((0, 0, 1), (2, 1, nodes - 1), (3, 2, nodes - 2), (1, 3, 0)):
        flight[k, "diag"] = wires.copy(
            terms.at[k, pl.ds(diag * tq, tq)], tnear.at[k, pl.ds(0, tq)], "rep", sib
        )
        flight[k, "sib"] = wires.copy(
            terms.at[k, pl.ds(sib * tq, tq)], tnear.at[k, pl.ds(tq, tq)], "rep", sib
        )
        flight[k, "x"] = wires.copy(tout.at[k], tfar.at[k], "rep", across)
        if d:
            flight[k, "late"] = wires.copy(lleave.at[j], lgot.at[j], "node", to_node(d))
            flight[k, "node"] = wires.copy(leaving.at[j], got.at[j], "node", to_node(d))
    wflight = {
        "x": wires.copy(wout, wfar, "rep", across),
        "over": wires.copy(wfull.at[me], wfull.at[me], "rep", across),
        "side": wires.copy(wfull.at[me], wfull.at[me], "rep", sib),
        "relay": wires.copy(wfull.at[across], wfull.at[across], "rep", sib),
    }
    for i, partner in enumerate(partners):
        wflight[i] = wires.copy(wstep.at[i], wgot.at[i], "node", partner)

    def terms_out(k):
        for r in range(count):
            terms[k, r] = ends(1, k, r).astype(BF16)
        flight[k, "diag"].start()
        flight[k, "sib"].start()

    def terms_cross(k, j, d):
        flight[k, "diag"].wait()
        for i in range(tq):
            value = terms[k, across * tq + i].astype(F32) + tnear[k, i].astype(F32)
            if i < EARLY:
                tout[k, i] = value.astype(BF16)
            elif d:
                lleave[j, i - EARLY] = value.astype(BF16)
            else:
                total[tq + i - EARLY] = value
        flight[k, "x"].start()
        if d:
            flight[k, "late"].start()

    def terms_leave(k, j, d):
        flight[k, "sib"].wait()
        flight[k, "x"].wait()
        for i in range(tq):
            value = terms[k, me * tq + i].astype(F32) + tnear[k, tq + i].astype(F32)
            if i < EARLY:
                value = value + tfar[k, i].astype(F32)
            if d:
                leaving[j, i] = value.astype(BF16)
            else:
                total[i] = value
        if d:
            flight[k, "node"].start()

    def wgrad_cross():
        for copy in wsib:
            copy.wait()
        wout[...] = (wmine[across].astype(F32) + wnear[0].astype(F32)).astype(BF16)
        wflight["x"].start()

    def wgrad_double(i):
        if i == 0:
            wflight["x"].wait()
            value = wmine[me].astype(F32) + wnear[1].astype(F32) + wfar[...].astype(F32)
        else:
            wflight[i - 1].wait()
            value = wstep[i - 1].astype(F32) + wgot[i - 1].astype(F32)
        if i < len(doubling):
            wstep[i] = value.astype(BF16)
            wflight[i].start()
        else:
            wfull[me] = (value * scale).astype(BF16)
            wflight["over"].start()
            wflight["side"].start()

    def wgrad_relay():
        wflight["over"].wait()
        wflight["relay"].start()

    C = lambda k, j, d: (lambda: terms_cross(k, j, d))
    L = lambda k, j, d: (lambda: terms_leave(k, j, d))
    W = lambda i: (lambda: wgrad_double(i))
    leg = {0: (0, 0, 1), 2: (2, 1, nodes - 1), 3: (3, 2, nodes - 2), 1: (1, 3, 0)}
    sweep(1, 0, full, [[], [], [wgrad_cross], []])
    terms_out(0)
    sweep(1, 2, full, [[], [C(*leg[0])], [W(0)], []])
    terms_out(2)
    sweep(1, 3, full, [[], [C(*leg[2])], [W(1)], []])
    terms_out(3)
    sweep(1, 1, full, [[L(*leg[0])], [C(*leg[3])], [W(2)], []])
    terms_out(1)
    terms_leave(*leg[2])
    terms_cross(*leg[1])
    for i in range(3, len(doubling) + 1):
        wgrad_double(i)
    terms_leave(*leg[3])
    spare = [total[tq + i] for i in range(late)]
    for j, k in enumerate((0, 2, 3)):
        flight[k, "late"].wait()
        spare = [spare[i] + lgot[j, i].astype(F32) for i in range(late)]
    for i in range(late):
        lout[i] = spare[i].astype(BF16)
    last_cross = wires.hop(lout, lfar, "rep", across)
    wgrad_relay()
    terms_leave(*leg[1])
    wflight["side"].wait()
    wflight["relay"].wait()
    for q in range(4):
        wgrad[q * wrows : (q + 1) * wrows, :] = wfull[q].astype(F32)
    for k in (0, 2, 3):
        flight[k, "node"].wait()
    last_cross.wait()
    values = []
    for i in range(tq):
        value = total[i]
        for j in range(3):
            value = value + got[j, i].astype(F32)
        if i >= EARLY:
            value = value + lfar[i - EARLY].astype(F32)
        values.append(value.astype(BF16))
    grad[...] = jnp.dot(
        pick[...], jnp.concatenate(values, axis=0), preferred_element_type=F32
    ).astype(grad.dtype)


def fused_call(nodes, scale, table, tiles, features, order, cot, weight):
    capacity, size = tiles.shape[1], tiles.shape[-1]
    feat = features.shape[1]
    count = features.shape[0] // size
    tq = count // 4
    late = tq - EARLY
    pairs = (capacity + count) // 2
    steps = nodes.bit_length() - 1
    vmem = pl.BlockSpec(memory_space=pltpu.VMEM)

    def rows(*lead):
        return pltpu.VMEM(lead + (size, feat), BF16)

    def sums(*lead):
        return pltpu.VMEM(lead + (size, feat), F32)

    def wide(*lead):
        return pltpu.VMEM(lead + (feat // 4, feat), BF16)

    flat = pltpu.VMEM((tq * size, feat), BF16)
    return pl.pallas_call(
        functools.partial(fused_kernel, nodes, scale),
        out_shape=(
            jax.ShapeDtypeStruct(cot.shape, BF16),
            jax.ShapeDtypeStruct(cot.shape, BF16),
            jax.ShapeDtypeStruct((feat, feat), F32),
        ),
        in_specs=[pl.BlockSpec(memory_space=pltpu.SMEM), pl.BlockSpec(memory_space=pl.ANY)]
        + [vmem] * 4,
        out_specs=(vmem,) * 3,
        scratch_shapes=[
            pltpu.VMEM((4, capacity + 1, size, size), BF16),
            rows(count), rows(count), rows(count), rows(count),
            sums(pairs + 1), sums(count),
            rows(count), rows(2 * tq), rows(tq), rows(tq), flat, flat, rows(count),
            rows(4, count), rows(4, 2 * tq), rows(4, EARLY), rows(4, EARLY),
            rows(3, tq), rows(3, tq), rows(3, late), rows(3, late),
            sums(tq + late), rows(late), rows(late),
            wide(4), wide(2), wide(), wide(), wide(steps), wide(steps), wide(4),
            pltpu.VMEM((tq * size, tq * size), BF16),
            pltpu.SemaphoreType.DMA((4,)),
            pltpu.SemaphoreType.DMA((128,)),
            pltpu.SemaphoreType.DMA((128,)),
        ],
        compiler_params=pltpu.CompilerParams(
            collective_id=0, has_side_effects=True, vmem_limit_bytes=60 * 1024 * 1024
        ),
    )(table, tiles, features, order, cot, weight)


def local(features, tiles, tile_rows, tile_cols, tile_count, order, weight, cotangent):
    nodes = lax.axis_size("node")
    size = tiles.shape[-1]
    scale = 1.0 / math.sqrt(features.shape[0] * nodes)
    table = table_call(tile_count.reshape(-1), tile_rows[0, 0], tile_cols[0, 0])
    activated, feature_grad, weight_grad = fused_call(
        nodes, scale, table, tiles[0, 0], features, order.reshape(-1, size), cotangent, weight
    )
    return (activated, feature_grad, weight_grad)


def solution(mesh):
    placed = (
        P("node", None),
        P("node", "rep", None, None, None, None),
        P("node", "rep", None, None),
        P("node", "rep", None, None),
        P("node", "rep", None),
        P("node"),
        P(),
        P(("node", "rep"), None),
    )
    return jax.shard_map(
        local,
        mesh=mesh,
        in_specs=placed,
        out_specs=(P(("node", "rep"), None), P(("node", "rep"), None), P()),
        check_vma=False,
    )
```

```python
import functools
import math

import jax
import jax.numpy as jnp
from jax import lax
from jax.experimental import pallas as pl
from jax.experimental.pallas import tpu as pltpu
from jax.sharding import PartitionSpec as P

EXCL = 3
SHARED = 2
EARLY = 3
GROUP = 14
VLIM = 60
FIELDS = 4
F32 = jnp.float32
BF16 = jnp.bfloat16


def table_kernel(capacity, count_src, row_src, col_src, out, stage, count_ref, rows, cols, sems):
    copies = [
        pltpu.make_async_copy(src, dst, sems.at[i])
        for i, (src, dst) in enumerate(((count_src, count_ref), (row_src, rows), (col_src, cols)))
    ]
    for copy in copies:
        copy.start()
    for copy in copies:
        copy.wait()
    lanes = stage.shape[1]
    stage[...] = jnp.zeros_like(stage)
    stage[0:4, 0:capacity] = rows[...].astype(F32)
    stage[4:8, 0:capacity] = cols[...].astype(F32)
    by_slot = stage[...].T
    sub = lax.broadcasted_iota(jnp.int32, (lanes, lanes), 0)
    lane = lax.broadcasted_iota(jnp.int32, (lanes, lanes), 1)
    lane_f = lane.astype(F32)
    before = (lane < sub).astype(BF16)
    upper = (sub < lane).astype(BF16)
    head = lax.broadcasted_iota(jnp.int32, (8, lanes), 0)
    for way in range(2):
        for k in range(4):
            key = by_slot[:, way * 4 + k : way * 4 + k + 1]
            live = sub < count_ref[0, k]
            mine = jnp.where(live & (key == lane_f), 1.0, 0.0)
            ahead = jnp.dot(before, mine.astype(BF16), preferred_element_type=F32)
            held = jnp.sum(mine, axis=0, keepdims=True)
            pairs = jnp.floor((held + 1.0) * 0.5)
            base = jnp.dot(
                jnp.broadcast_to(pairs, (8, lanes)).astype(BF16), upper, preferred_element_type=F32
            )[0:1]
            rank = jnp.sum(mine * ahead, axis=1, keepdims=True)
            spot = jnp.sum(mine * (2.0 * base), axis=1, keepdims=True) + rank
            put = jnp.where(live & (spot == lane_f), 1.0, 0.0)
            starts = jnp.sum(jnp.where(rank == 0.0, put, 0.0), axis=0, keepdims=True)
            other = stage[(1 - way) * 4 + k : (1 - way) * 4 + k + 1, :]
            values = jnp.where(
                head == 0, lane_f[0:8], jnp.where(head == 1, jnp.broadcast_to(other, (8, lanes)), 1.0)
            )
            found = jnp.dot(values.astype(BF16), put.astype(BF16), preferred_element_type=F32)
            slot = jnp.where(found[2:3] > 0.0, found[0:1], float(capacity))
            last = jnp.where(held > 0.0, base + pairs, 0.0)
            at = (way * 4 + k) * FIELDS
            out[at : at + 1, :] = slot.astype(jnp.int32)
            out[at + 1 : at + 2, :] = found[1:2].astype(jnp.int32)
            out[at + 2 : at + 3, :] = (1.0 - starts).astype(jnp.int32)
            out[at + 3 : at + 4, :] = last.astype(jnp.int32)


def table_call(counts, row_ids, col_ids):
    capacity = row_ids.shape[-1]
    return pl.pallas_call(
        functools.partial(table_kernel, capacity),
        out_shape=jax.ShapeDtypeStruct((8 * FIELDS, 128), jnp.int32),
        in_specs=[pl.BlockSpec(memory_space=pl.ANY)] * 3,
        out_specs=pl.BlockSpec(memory_space=pltpu.VMEM),
        scratch_shapes=[
            pltpu.VMEM((128, 128), F32),
            pltpu.SMEM(counts.shape, jnp.int32),
            pltpu.VMEM(row_ids.shape, jnp.int32),
            pltpu.VMEM(col_ids.shape, jnp.int32),
            pltpu.SemaphoreType.DMA((3,)),
        ],
        compiler_params=pltpu.CompilerParams(vmem_limit_bytes=VLIM * 1024 * 1024),
    )(counts, row_ids, col_ids)


class Wires:
    def __init__(self, send, recv):
        self.send, self.recv, self.used = send, recv, 0

    def copy(self, src, dst, axis, target):
        at = self.used
        self.used += 1
        return pltpu.make_async_remote_copy(
            src_ref=src,
            dst_ref=dst,
            send_sem=self.send.at[at],
            recv_sem=self.recv.at[at],
            device_id={axis: target},
            device_id_type=pl.DeviceIdType.MESH,
        )

    def hop(self, src, dst, axis, target):
        copy = self.copy(src, dst, axis, target)
        copy.start()
        return copy


def fused_kernel(
    nodes, scale, table, tiles, feature_src, order_src, cot_src, weight_src,
    act, grad, wgrad, features, order, cot, weight,
    held, here, halo_a, halo_b, halo_c, sums, acc, part, near, outgoing, far, agg, pg, full,
    terms, tnear, tout, tfar, leaving, got, lleave, lgot, total, lout, lfar,
    wmine, wnear, wout, wfar, wstep, wgot, wfull, pick,
    load_sems, stage_sems, send, recv,
):
    capacity = tiles.shape[1]
    count, size, feat = here.shape
    tq = count // 4
    quarter = tq * size
    pairs = (capacity + count) // 2
    me, home = lax.axis_index("rep"), lax.axis_index("node")
    x, c = me // 2, me % 2
    sib, across, diag = x * 2 + 1 - c, (1 - x) * 2 + c, (1 - x) * 2 + 1 - c
    wires = Wires(send, recv)

    def to_node(d):
        return (home + d) % nodes

    doubling = [1 << i for i in range(nodes.bit_length() - 1)]
    partners = []
    for step in doubling:
        low = (home // step) % 2
        partners.append(home + step - 2 * step * low)
    peers = [("rep", sib), ("rep", across)]
    peers += [("node", to_node(d)) for d in (1, nodes - 1, 2, nodes - 2)]
    peers += [("node", p) for p in partners]
    barrier = pltpu.get_barrier_semaphore()
    for axis, target in peers:
        pl.semaphore_signal(
            barrier, inc=1, device_id={axis: target}, device_id_type=pl.DeviceIdType.MESH
        )

    staged = [
        pltpu.make_async_copy(src, dst, stage_sems.at[i])
        for i, (src, dst) in enumerate(
            (
                (order_src, order), (feature_src, features), (cot_src, cot), (weight_src, weight),
            )
        )
    ]
    for copy in staged:
        copy.start()
    loads = [
        pltpu.make_async_copy(
            tiles.at[k], held.at[k, pl.ds(0, capacity)], load_sems.at[k]
        )
        for k in (1, 0, 2, 3)
    ]
    for load in loads:
        load.start()

    spots = lax.broadcasted_iota(jnp.int32, (quarter, size), 0)

    def chosen(t):
        return (spots == lax.rem(order[pl.ds(t, 1), :], quarter)).astype(BF16)

    def reorder(t):
        rows = features[pl.ds(pl.multiple_of((t // tq) * quarter, quarter), quarter), :]
        here[t] = lax.dot_general(
            chosen(t), rows, (((0,), (0,)), ((), ())), preferred_element_type=F32
        ).astype(BF16)

    first = 10 * x + EXCL * c
    common = 2 * 2 * EXCL // 2 + SHARED * c
    other = 10 * (1 - x) + EXCL * c
    for copy in staged[:2]:
        copy.wait()
    for i in range(EXCL):
        reorder(first + i)
    for i in range(SHARED):
        reorder(common + i)
    pl.semaphore_wait(barrier, len(peers))

    moves = ((2, halo_a), (nodes - 1, halo_b), (1, halo_c))
    direct, shared = [], []
    for d, land in moves:
        direct.append(
            [
                wires.hop(here.at[first + i], land.at[first + i], "node", to_node(d))
                for i in range(EXCL)
            ]
        )
        block = pl.ds(common, SHARED)
        shared.append(wires.hop(here.at[block], land.at[block], "node", to_node(d)))
    for i in range(EXCL):
        reorder(other + i)
    rest = 10 * x + EXCL * (1 - c)
    for i in range(EXCL):
        reorder(rest + i)
        reorder(10 * (1 - x) + EXCL * (1 - c) + i)
    for i in range(SHARED):
        reorder(2 * EXCL + SHARED * (1 - c) + i)
    for copy in staged[2:]:
        copy.wait()
    for k in range(4):
        held[k, capacity] = jnp.zeros((size, size), BF16)
    sums[0] = jnp.zeros((size, feat), F32)
    mine_pick = jnp.concatenate([chosen(me * tq + i) for i in range(tq)], axis=1)
    pick[...] = mine_pick

    crossing, aside_direct, aside_cross, aside_shared = [], [], [], []
    for d, land in moves:
        for i in range(EXCL):
            near_tile, far_tile = land.at[first + i], land.at[other + i]
            crossing.append(wires.copy(near_tile, near_tile, "rep", across))
            aside_direct.append(wires.copy(near_tile, near_tile, "rep", sib))
            aside_cross.append(wires.copy(far_tile, far_tile, "rep", sib))
        both = land.at[pl.ds(common, SHARED)]
        aside_shared.append(wires.copy(both, both, "rep", sib))

    def event_direct(g):
        direct[g // EXCL][g % EXCL].wait()
        crossing[g].start()
        aside_direct[g].start()

    def event_cross(g):
        crossing[g].wait()
        aside_cross[g].start()

    def event_shared(j):
        shared[j].wait()
        aside_shared[j].start()

    def settle(j):
        for i in range(EXCL):
            aside_direct[j * EXCL + i].wait()
            aside_cross[j * EXCL + i].wait()
        aside_shared[j].wait()

    def product(way, k, i, source):
        at = (way * 4 + k) * FIELDS
        one, two = held[k, table[at, 2 * i]], held[k, table[at, 2 * i + 1]]
        left, right = source[table[at + 1, 2 * i]], source[table[at + 1, 2 * i + 1]]
        rows = jnp.concatenate([left, right], axis=0)
        if way == 0:
            return jnp.dot(
                jnp.concatenate([one, two], axis=1), rows, preferred_element_type=F32
            )
        return lax.dot_general(
            jnp.concatenate([one, two], axis=0), rows, (((0,), (0,)), ((), ())),
            preferred_element_type=F32,
        )

    def sweep(way, k, source, events):
        at = (way * 4 + k) * FIELDS

        def body(step, _):
            for turn, work in enumerate(events):
                if work:
                    @pl.when(step == turn)
                    def _(work=work):
                        for f in work:
                            f()
            base = step * GROUP
            products = [product(way, k, base + g, source) for g in range(GROUP)]
            value = sums[base]
            for g in range(GROUP):
                value = products[g] + table[at + 2, 2 * (base + g)].astype(F32) * value
                sums[base + g + 1] = value
            return 0

        lax.fori_loop(0, pairs // GROUP, body, 0)

    def ends(way, k, r):
        return sums[table[(way * 4 + k) * FIELDS + 3, r]]

    def run(*work):
        for f in work:
            f()

    E = lambda g: (lambda: event_direct(g))
    X = lambda g: (lambda: event_cross(g))
    S = lambda j: (lambda: event_shared(j))

    for load in loads:
        load.wait()
    sweep(0, 1, here, [[E(0)], [E(1)], [E(2), X(0)], [E(3), X(1)]])
    for r in range(count):
        acc[r] = ends(0, 1, r)
    run(E(4), X(2), S(0))
    settle(0)
    sweep(0, 3, halo_a, [[E(5), X(3)], [E(6), X(4)], [E(7), X(5)], [E(8), X(6)]])
    for r in range(count):
        acc[r] += ends(0, 3, r)
    run(S(1))
    settle(1)
    sweep(0, 0, halo_b, [[X(7)], [X(8), S(2)], [], []])
    for r in range(count):
        acc[r] += ends(0, 0, r)
    settle(2)
    sweep(0, 2, halo_c, [[], [], [], []])

    def finish_rows(q):
        for i in range(tq):
            r = q * tq + i
            value = acc[r] + ends(0, 2, r)
            acc[r] = value
            part[r] = value.astype(BF16)

    finish_rows(diag)
    to_sib = [
        wires.hop(part.at[diag * tq + i], near.at[i], "rep", sib) for i in range(tq)
    ]
    finish_rows(sib)
    block = pl.ds(sib * tq, tq)
    rest_sib = wires.hop(part.at[block], near.at[pl.ds(tq, tq)], "rep", sib)
    finish_rows(across)
    crossed = []
    for i in range(tq):
        to_sib[i].wait()
        outgoing[i] = (acc[across * tq + i] + near[i].astype(F32)).astype(BF16)
        crossed.append(wires.hop(outgoing.at[i], far.at[i], "rep", across))
    finish_rows(me)
    rest_sib.wait()
    over, side, relay = [], [], []
    for i in range(tq):
        r = me * tq + i
        mine = acc[r] + near[tq + i].astype(F32)
        crossed[i].wait()
        aggregate = (mine + far[i].astype(F32)).astype(BF16)
        agg[i * size : (i + 1) * size, :] = aggregate
        pre_act = jnp.dot(aggregate, weight[...], preferred_element_type=F32)
        gate = jax.nn.sigmoid(pre_act)
        act[i * size : (i + 1) * size, :] = (pre_act * gate).astype(act.dtype)
        pre_grad = (
            cot[i * size : (i + 1) * size, :].astype(F32) * gate * (1.0 + pre_act * (1.0 - gate))
        ).astype(BF16)
        pg[i * size : (i + 1) * size, :] = pre_grad
        full[r] = lax.dot_general(
            pre_grad, weight[...], (((1,), (1,)), ((), ())), preferred_element_type=F32
        ).astype(BF16)
        over.append(wires.hop(full.at[r], full.at[r], "rep", across))
        side.append(wires.hop(full.at[r], full.at[r], "rep", sib))
    wrows = feat // 4
    wpart = lax.dot_general(
        agg[...], pg[...], (((0,), (0,)), ((), ())), preferred_element_type=F32
    )
    for q in range(4):
        wmine[q] = wpart[q * wrows : (q + 1) * wrows, :].astype(BF16)
    for i in range(tq):
        over[i].wait()
        r = across * tq + i
        relay.append(wires.hop(full.at[r], full.at[r], "rep", sib))
    wsib = [
        wires.hop(wmine.at[diag], wnear.at[0], "rep", sib),
        wires.hop(wmine.at[sib], wnear.at[1], "rep", sib),
    ]
    for copy in side + relay:
        copy.wait()

    late = tq - EARLY
    flight = {}
    for k, j, d in ((0, 0, 1), (2, 1, nodes - 1), (3, 2, nodes - 2), (1, 3, 0)):
        flight[k, "diag"] = wires.copy(
            terms.at[k, pl.ds(diag * tq, tq)], tnear.at[k, pl.ds(0, tq)], "rep", sib
        )
        flight[k, "sib"] = wires.copy(
            terms.at[k, pl.ds(sib * tq, tq)], tnear.at[k, pl.ds(tq, tq)], "rep", sib
        )
        for i in range(EARLY):
            flight[k, "x", i] = wires.copy(tout.at[k, i], tfar.at[k, i], "rep", across)
        if d:
            flight[k, "late"] = wires.copy(lleave.at[j], lgot.at[j], "node", to_node(d))
            for i in range(EARLY):
                flight[k, "node", i] = wires.copy(
                    leaving.at[j, i], got.at[j, i], "node", to_node(d)
                )
            tail = pl.ds(EARLY, late)
            flight[k, "node", EARLY] = wires.copy(
                leaving.at[j, tail], got.at[j, tail], "node", to_node(d)
            )
    wflight = {
        "x": wires.copy(wout, wfar, "rep", across),
        "over": wires.copy(wfull.at[me], wfull.at[me], "rep", across),
        "side": wires.copy(wfull.at[me], wfull.at[me], "rep", sib),
        "relay": wires.copy(wfull.at[across], wfull.at[across], "rep", sib),
    }
    for i, partner in enumerate(partners):
        wflight[i] = wires.copy(wstep.at[i], wgot.at[i], "node", partner)

    def terms_out(k):
        for q, name in ((diag, "diag"), (sib, "sib"), (across, None), (me, None)):
            for i in range(tq):
                r = q * tq + i
                terms[k, r] = ends(1, k, r).astype(BF16)
            if name:
                flight[k, name].start()

    def terms_cross(k, j, d):
        flight[k, "diag"].wait()
        for i in range(tq):
            value = terms[k, across * tq + i].astype(F32) + tnear[k, i].astype(F32)
            if i < EARLY:
                tout[k, i] = value.astype(BF16)
                flight[k, "x", i].start()
            elif d:
                lleave[j, i - EARLY] = value.astype(BF16)
            else:
                total[tq + i - EARLY] = value
        if d:
            flight[k, "late"].start()
        flight[k, "sib"].wait()
        for i in range(EARLY, tq):
            value = terms[k, me * tq + i].astype(F32) + tnear[k, tq + i].astype(F32)
            if d:
                leaving[j, i] = value.astype(BF16)
            else:
                total[i] = value
        if d:
            flight[k, "node", EARLY].start()

    def terms_leave(k, j, d, i):
        flight[k, "x", i].wait()
        value = terms[k, me * tq + i].astype(F32) + tnear[k, tq + i].astype(F32)
        value = value + tfar[k, i].astype(F32)
        if d:
            leaving[j, i] = value.astype(BF16)
            flight[k, "node", i].start()
        else:
            total[i] = value

    def wgrad_cross():
        for copy in wsib:
            copy.wait()
        wout[...] = (wmine[across].astype(F32) + wnear[0].astype(F32)).astype(BF16)
        wflight["x"].start()

    def wgrad_double(i):
        if i == 0:
            wflight["x"].wait()
            value = wmine[me].astype(F32) + wnear[1].astype(F32) + wfar[...].astype(F32)
        else:
            wflight[i - 1].wait()
            value = wstep[i - 1].astype(F32) + wgot[i - 1].astype(F32)
        if i < len(doubling):
            wstep[i] = value.astype(BF16)
            wflight[i].start()
        else:
            wfull[me] = (value * scale).astype(BF16)
            wflight["over"].start()
            wflight["side"].start()

    def wgrad_relay():
        wflight["over"].wait()
        wflight["relay"].start()

    C = lambda k, j, d: (lambda: terms_cross(k, j, d))
    L = lambda k, j, d, i: (lambda: terms_leave(k, j, d, i))
    W = lambda i: (lambda: wgrad_double(i))
    leg = {0: (0, 0, 1), 2: (2, 1, nodes - 1), 3: (3, 2, nodes - 2), 1: (1, 3, 0)}
    sweep(1, 3, full, [[], [], [wgrad_cross], []])
    terms_out(3)
    sweep(1, 0, full, [[], [C(*leg[3])], [W(0)], []])
    terms_out(0)
    sweep(1, 2, full, [[], [C(*leg[0])], [W(1)], []])
    terms_out(2)
    sweep(1, 1, full, [[L(*leg[3], 0)], [C(*leg[2]), L(*leg[3], 1)], [W(2), L(*leg[3], 2)], []])
    terms_out(1)
    terms_leave(*leg[0], 0)
    terms_cross(*leg[1])
    for i in range(1, EARLY):
        terms_leave(*leg[0], i)
    for i in range(3, len(doubling) + 1):
        wgrad_double(i)
    for i in range(EARLY):
        terms_leave(*leg[2], i)
    spare = [total[tq + i] for i in range(late)]
    for j, k in enumerate((0, 2, 3)):
        flight[k, "late"].wait()
        spare = [spare[i] + lgot[j, i].astype(F32) for i in range(late)]
    for i in range(late):
        lout[i] = spare[i].astype(BF16)
    last_cross = wires.hop(lout, lfar, "rep", across)
    wgrad_relay()
    for i in range(EARLY):
        terms_leave(*leg[1], i)
    wflight["side"].wait()
    wflight["relay"].wait()
    for q in range(4):
        wgrad[q * wrows : (q + 1) * wrows, :] = wfull[q].astype(F32)
    for k in (0, 2, 3):
        for i in range(EARLY + 1):
            flight[k, "node", i].wait()
    last_cross.wait()
    values = []
    for i in range(tq):
        value = total[i]
        for j in range(3):
            value = value + got[j, i].astype(F32)
        if i >= EARLY:
            value = value + lfar[i - EARLY].astype(F32)
        values.append(value.astype(BF16))
    grad[...] = jnp.dot(
        pick[...], jnp.concatenate(values, axis=0), preferred_element_type=F32
    ).astype(grad.dtype)


def fused_call(nodes, scale, table, tiles, features, order, cot, weight):
    capacity, size = tiles.shape[1], tiles.shape[-1]
    feat = features.shape[1]
    count = features.shape[0] // size
    tq = count // 4
    late = tq - EARLY
    pairs = (capacity + count) // 2
    steps = nodes.bit_length() - 1
    vmem = pl.BlockSpec(memory_space=pltpu.VMEM)

    def rows(*lead):
        return pltpu.VMEM(lead + (size, feat), BF16)

    def sums(*lead):
        return pltpu.VMEM(lead + (size, feat), F32)

    def wide(*lead):
        return pltpu.VMEM(lead + (feat // 4, feat), BF16)

    flat = pltpu.VMEM((tq * size, feat), BF16)
    return pl.pallas_call(
        functools.partial(fused_kernel, nodes, scale),
        out_shape=(
            jax.ShapeDtypeStruct(cot.shape, BF16),
            jax.ShapeDtypeStruct(cot.shape, BF16),
            jax.ShapeDtypeStruct((feat, feat), F32),
        ),
        in_specs=[pl.BlockSpec(memory_space=pltpu.SMEM)] + [pl.BlockSpec(memory_space=pl.ANY)] * 5,
        out_specs=(vmem,) * 3,
        scratch_shapes=[
            pltpu.VMEM(features.shape, BF16),
            pltpu.VMEM(order.shape, jnp.int32),
            pltpu.VMEM(cot.shape, BF16),
            pltpu.VMEM(weight.shape, BF16),
            pltpu.VMEM((4, capacity + 1, size, size), BF16),
            rows(count), rows(count), rows(count), rows(count),
            sums(pairs + 1), sums(count),
            rows(count), rows(2 * tq), rows(tq), rows(tq), flat, flat, rows(count),
            rows(4, count), rows(4, 2 * tq), rows(4, EARLY), rows(4, EARLY),
            rows(3, tq), rows(3, tq), rows(3, late), rows(3, late),
            sums(tq + late), rows(late), rows(late),
            wide(4), wide(2), wide(), wide(), wide(steps), wide(steps), wide(4),
            pltpu.VMEM((tq * size, tq * size), BF16),
            pltpu.SemaphoreType.DMA((4,)),
            pltpu.SemaphoreType.DMA((4,)),
            pltpu.SemaphoreType.DMA((128,)),
            pltpu.SemaphoreType.DMA((128,)),
        ],
        compiler_params=pltpu.CompilerParams(
            collective_id=0, has_side_effects=True, vmem_limit_bytes=VLIM * 1024 * 1024
        ),
    )(table, tiles, features, order, cot, weight)


def publish_kernel(*refs):
    n = (len(refs) - 2) // 3
    ins, outs, held = refs[:n], refs[n : 2 * n], refs[2 * n : 3 * n]
    take, give = refs[3 * n], refs[3 * n + 1]
    loads = [pltpu.make_async_copy(ins[i], held[i], take.at[i]) for i in range(n)]
    stores = [pltpu.make_async_copy(held[i], outs[i], give.at[i]) for i in range(n)]
    for load in loads:
        load.start()
    for load, store in zip(loads, stores):
        load.wait()
        store.start()
    for store in stores:
        store.wait()


def publish_call(*arrays):
    n = len(arrays)
    return pl.pallas_call(
        publish_kernel,
        out_shape=tuple(jax.ShapeDtypeStruct(a.shape, a.dtype) for a in arrays),
        in_specs=[pl.BlockSpec(memory_space=pl.ANY)] * n,
        out_specs=(pl.BlockSpec(memory_space=pl.ANY),) * n,
        scratch_shapes=[pltpu.VMEM(a.shape, a.dtype) for a in arrays]
        + [pltpu.SemaphoreType.DMA((n,))] * 2,
        compiler_params=pltpu.CompilerParams(vmem_limit_bytes=VLIM * 1024 * 1024),
    )(*arrays)


def local(features, tiles, tile_rows, tile_cols, tile_count, order, weight, cotangent):
    nodes = lax.axis_size("node")
    size = tiles.shape[-1]
    scale = 1.0 / math.sqrt(features.shape[0] * nodes)
    table = table_call(tile_count[0], tile_rows[0, 0], tile_cols[0, 0])
    outs = fused_call(
        nodes, scale, table, tiles[0, 0], features, order.reshape(-1, size), cotangent, weight
    )
    return publish_call(*outs)


def solution(mesh):
    placed = (
        P("node", None),
        P("node", "rep", None, None, None, None),
        P("node", "rep", None, None),
        P("node", "rep", None, None),
        P("node", "rep", None),
        P("node"),
        P(),
        P(("node", "rep"), None),
    )
    return jax.shard_map(
        local,
        mesh=mesh,
        in_specs=placed,
        out_specs=(P(("node", "rep"), None), P(("node", "rep"), None), P()),
        check_vma=False,
    )
```

```python
import functools
import math

import jax
import jax.numpy as jnp
from jax import lax
from jax.experimental import pallas as pl
from jax.experimental.pallas import tpu as pltpu
from jax.sharding import PartitionSpec as P

EXCL = 3
SHARED = 2
EARLY = 3
GROUP = 14
VLIM = 60
FIELDS = 4
F32 = jnp.float32
BF16 = jnp.bfloat16


def sort_slots(capacity, count_ref, rows, cols, out, stage):
    lanes = stage.shape[1]
    zero = jnp.int32(0)
    stage[...] = jnp.zeros_like(stage)
    stage[0:4, 0:capacity] = rows[...]
    stage[4:8, 0:capacity] = cols[...]
    by_slot = stage[...].T
    sub = lax.broadcasted_iota(jnp.int32, (capacity, lanes), 0)
    lane = lax.broadcasted_iota(jnp.int32, (capacity, lanes), 1)
    for way in range(2):
        for k in range(4):
            at, pick = (way * 4 + k) * FIELDS, way * 4 + k
            key = by_slot[0:capacity, pick : pick + 1]
            other = by_slot[0:capacity, (1 - way) * 4 + k : (1 - way) * 4 + k + 1]
            along = stage[pick : pick + 1, :]
            live = sub < count_ref[0, k]
            same = live & (key == along) & (lane < sub)
            rank = jnp.sum(jnp.where(same, 1, zero), axis=1, keepdims=True)
            held = jnp.sum(jnp.where(live & (key == lane), 1, zero), axis=0, keepdims=True)
            odd = held - 2 * lax.shift_right_logical(held, 1)
            padded = held + odd
            base = jnp.sum(jnp.where(lane < key, padded, zero), axis=1, keepdims=True)
            length = jnp.sum(jnp.where(lane == key, padded, zero), axis=1, keepdims=True)
            spot = base + rank
            put = live & (spot == lane)
            slot = jnp.sum(jnp.where(put, sub - capacity, zero), axis=0, keepdims=True)
            source = jnp.sum(jnp.where(put, other, zero), axis=0, keepdims=True)
            starts = jnp.sum(jnp.where(put & (rank == 0), 1, zero), axis=0, keepdims=True)
            reach = jnp.where(live & (key == lane) & (rank == 0), base + length, zero)
            last = lax.shift_right_logical(jnp.sum(reach, axis=0, keepdims=True), 1)
            out[at : at + 1, :] = slot + capacity
            out[at + 1 : at + 2, :] = source
            out[at + 2 : at + 3, :] = 1 - starts
            out[at + 3 : at + 4, :] = last


class Wires:
    def __init__(self, send, recv):
        self.send, self.recv, self.used = send, recv, 0

    def copy(self, src, dst, axis, target):
        at = self.used
        self.used += 1
        return pltpu.make_async_remote_copy(
            src_ref=src,
            dst_ref=dst,
            send_sem=self.send.at[at],
            recv_sem=self.recv.at[at],
            device_id={axis: target},
            device_id_type=pl.DeviceIdType.MESH,
        )

    def hop(self, src, dst, axis, target):
        copy = self.copy(src, dst, axis, target)
        copy.start()
        return copy


def fused_kernel(
    nodes, scale, count_src, row_src, col_src, tiles, feature_src, order_src, cot_src, weight_src,
    act, grad, wgrad, count_ref, row_ids, col_ids, features, order, cot, weight,
    held, here, halo_a, halo_b, halo_c, sums, acc, part, near, outgoing, far, agg, pg, full,
    terms, tnear, tout, tfar, leaving, got, lleave, lgot, total, lout, lfar,
    wmine, wnear, wout, wfar, wstep, wgot, wfull, pick,
    stage, sorted_slots, table, load_sems, stage_sems, send, recv,
):
    capacity = tiles.shape[1]
    count, size, feat = here.shape
    tq = count // 4
    quarter = tq * size
    pairs = (capacity + count) // 2
    me, home = lax.axis_index("rep"), lax.axis_index("node")
    x, c = me // 2, me % 2
    sib, across, diag = x * 2 + 1 - c, (1 - x) * 2 + c, (1 - x) * 2 + 1 - c
    wires = Wires(send, recv)

    def to_node(d):
        return (home + d) % nodes

    doubling = [1 << i for i in range(nodes.bit_length() - 1)]
    partners = []
    for step in doubling:
        low = (home // step) % 2
        partners.append(home + step - 2 * step * low)
    peers = [("rep", sib), ("rep", across)]
    peers += [("node", to_node(d)) for d in (1, nodes - 1, 2, nodes - 2)]
    peers += [("node", p) for p in partners]
    barrier = pltpu.get_barrier_semaphore()
    for axis, target in peers:
        pl.semaphore_signal(
            barrier, inc=1, device_id={axis: target}, device_id_type=pl.DeviceIdType.MESH
        )

    staged = [
        pltpu.make_async_copy(src, dst, stage_sems.at[i])
        for i, (src, dst) in enumerate(
            (
                (order_src, order), (feature_src, features), (count_src, count_ref),
                (row_src, row_ids), (col_src, col_ids), (cot_src, cot), (weight_src, weight),
            )
        )
    ]
    for copy in staged:
        copy.start()
    loads = [
        pltpu.make_async_copy(
            tiles.at[k], held.at[k, pl.ds(0, capacity)], load_sems.at[k]
        )
        for k in (1, 0, 2, 3)
    ]
    for load in loads:
        load.start()

    spots = lax.broadcasted_iota(jnp.int32, (quarter, size), 0)

    def chosen(t):
        return (spots == lax.rem(order[pl.ds(t, 1), :], quarter)).astype(BF16)

    def reorder(t):
        rows = features[pl.ds(pl.multiple_of((t // tq) * quarter, quarter), quarter), :]
        here[t] = lax.dot_general(
            chosen(t), rows, (((0,), (0,)), ((), ())), preferred_element_type=F32
        ).astype(BF16)

    first = 10 * x + EXCL * c
    common = 2 * 2 * EXCL // 2 + SHARED * c
    other = 10 * (1 - x) + EXCL * c
    for copy in staged[:2]:
        copy.wait()
    for i in range(EXCL):
        reorder(first + i)
    for i in range(SHARED):
        reorder(common + i)
    pl.semaphore_wait(barrier, len(peers))

    moves = ((2, halo_a), (nodes - 1, halo_b), (1, halo_c))
    direct, shared = [], []
    for d, land in moves:
        direct.append(
            [
                wires.hop(here.at[first + i], land.at[first + i], "node", to_node(d))
                for i in range(EXCL)
            ]
        )
        block = pl.ds(common, SHARED)
        shared.append(wires.hop(here.at[block], land.at[block], "node", to_node(d)))
    for i in range(EXCL):
        reorder(other + i)
    rest = 10 * x + EXCL * (1 - c)
    for i in range(EXCL):
        reorder(rest + i)
        reorder(10 * (1 - x) + EXCL * (1 - c) + i)
    for i in range(SHARED):
        reorder(2 * EXCL + SHARED * (1 - c) + i)
    for copy in staged[2:]:
        copy.wait()
    sort_slots(capacity, count_ref, row_ids, col_ids, sorted_slots, stage)
    fetch = pltpu.make_async_copy(sorted_slots, table, load_sems.at[4])
    fetch.start()
    for k in range(4):
        held[k, capacity] = jnp.zeros((size, size), BF16)
    sums[0] = jnp.zeros((size, feat), F32)
    mine_pick = jnp.concatenate([chosen(me * tq + i) for i in range(tq)], axis=1)
    pick[...] = mine_pick

    crossing, aside_direct, aside_cross, aside_shared = [], [], [], []
    for d, land in moves:
        for i in range(EXCL):
            near_tile, far_tile = land.at[first + i], land.at[other + i]
            crossing.append(wires.copy(near_tile, near_tile, "rep", across))
            aside_direct.append(wires.copy(near_tile, near_tile, "rep", sib))
            aside_cross.append(wires.copy(far_tile, far_tile, "rep", sib))
        both = land.at[pl.ds(common, SHARED)]
        aside_shared.append(wires.copy(both, both, "rep", sib))

    def event_direct(g):
        direct[g // EXCL][g % EXCL].wait()
        crossing[g].start()
        aside_direct[g].start()

    def event_cross(g):
        crossing[g].wait()
        aside_cross[g].start()

    def event_shared(j):
        shared[j].wait()
        aside_shared[j].start()

    def settle(j):
        for i in range(EXCL):
            aside_direct[j * EXCL + i].wait()
            aside_cross[j * EXCL + i].wait()
        aside_shared[j].wait()

    def product(way, k, i, source):
        at = (way * 4 + k) * FIELDS
        one, two = held[k, table[at, 2 * i]], held[k, table[at, 2 * i + 1]]
        left, right = source[table[at + 1, 2 * i]], source[table[at + 1, 2 * i + 1]]
        rows = jnp.concatenate([left, right], axis=0)
        if way == 0:
            return jnp.dot(
                jnp.concatenate([one, two], axis=1), rows, preferred_element_type=F32
            )
        return lax.dot_general(
            jnp.concatenate([one, two], axis=0), rows, (((0,), (0,)), ((), ())),
            preferred_element_type=F32,
        )

    def sweep(way, k, source, events):
        at = (way * 4 + k) * FIELDS

        def body(step, _):
            for turn, work in enumerate(events):
                if work:
                    @pl.when(step == turn)
                    def _(work=work):
                        for f in work:
                            f()
            base = step * GROUP
            products = [product(way, k, base + g, source) for g in range(GROUP)]
            value = sums[base]
            for g in range(GROUP):
                value = products[g] + table[at + 2, 2 * (base + g)].astype(F32) * value
                sums[base + g + 1] = value
            return 0

        lax.fori_loop(0, pairs // GROUP, body, 0)

    def ends(way, k, r):
        return sums[table[(way * 4 + k) * FIELDS + 3, r]]

    def run(*work):
        for f in work:
            f()

    E = lambda g: (lambda: event_direct(g))
    X = lambda g: (lambda: event_cross(g))
    S = lambda j: (lambda: event_shared(j))

    fetch.wait()
    for load in loads:
        load.wait()
    sweep(0, 1, here, [[E(0)], [E(1)], [E(2), X(0)], [E(3), X(1)]])
    for r in range(count):
        acc[r] = ends(0, 1, r)
    run(E(4), X(2), S(0))
    settle(0)
    sweep(0, 3, halo_a, [[E(5), X(3)], [E(6), X(4)], [E(7), X(5)], [E(8), X(6)]])
    for r in range(count):
        acc[r] += ends(0, 3, r)
    run(S(1))
    settle(1)
    sweep(0, 0, halo_b, [[X(7)], [X(8), S(2)], [], []])
    for r in range(count):
        acc[r] += ends(0, 0, r)
    settle(2)
    sweep(0, 2, halo_c, [[], [], [], []])

    def finish_rows(q):
        for i in range(tq):
            r = q * tq + i
            value = acc[r] + ends(0, 2, r)
            acc[r] = value
            part[r] = value.astype(BF16)

    finish_rows(diag)
    to_sib = [
        wires.hop(part.at[diag * tq + i], near.at[i], "rep", sib) for i in range(tq)
    ]
    finish_rows(sib)
    block = pl.ds(sib * tq, tq)
    rest_sib = wires.hop(part.at[block], near.at[pl.ds(tq, tq)], "rep", sib)
    finish_rows(across)
    crossed = []
    for i in range(tq):
        to_sib[i].wait()
        outgoing[i] = (acc[across * tq + i] + near[i].astype(F32)).astype(BF16)
        crossed.append(wires.hop(outgoing.at[i], far.at[i], "rep", across))
    finish_rows(me)
    rest_sib.wait()
    over, side, relay = [], [], []
    for i in range(tq):
        r = me * tq + i
        mine = acc[r] + near[tq + i].astype(F32)
        crossed[i].wait()
        aggregate = (mine + far[i].astype(F32)).astype(BF16)
        agg[i * size : (i + 1) * size, :] = aggregate
        pre_act = jnp.dot(aggregate, weight[...], preferred_element_type=F32)
        gate = jax.nn.sigmoid(pre_act)
        act[i * size : (i + 1) * size, :] = (pre_act * gate).astype(act.dtype)
        pre_grad = (
            cot[i * size : (i + 1) * size, :].astype(F32) * gate * (1.0 + pre_act * (1.0 - gate))
        ).astype(BF16)
        pg[i * size : (i + 1) * size, :] = pre_grad
        full[r] = lax.dot_general(
            pre_grad, weight[...], (((1,), (1,)), ((), ())), preferred_element_type=F32
        ).astype(BF16)
        over.append(wires.hop(full.at[r], full.at[r], "rep", across))
        side.append(wires.hop(full.at[r], full.at[r], "rep", sib))
    wrows = feat // 4
    wpart = lax.dot_general(
        agg[...], pg[...], (((0,), (0,)), ((), ())), preferred_element_type=F32
    )
    for q in range(4):
        wmine[q] = wpart[q * wrows : (q + 1) * wrows, :].astype(BF16)
    for i in range(tq):
        over[i].wait()
        r = across * tq + i
        relay.append(wires.hop(full.at[r], full.at[r], "rep", sib))
    wsib = [
        wires.hop(wmine.at[diag], wnear.at[0], "rep", sib),
        wires.hop(wmine.at[sib], wnear.at[1], "rep", sib),
    ]
    for copy in side + relay:
        copy.wait()

    late = tq - EARLY
    flight = {}
    for k, j, d in ((0, 0, 1), (2, 1, nodes - 1), (3, 2, nodes - 2), (1, 3, 0)):
        flight[k, "diag"] = wires.copy(
            terms.at[k, pl.ds(diag * tq, tq)], tnear.at[k, pl.ds(0, tq)], "rep", sib
        )
        flight[k, "sib"] = wires.copy(
            terms.at[k, pl.ds(sib * tq, tq)], tnear.at[k, pl.ds(tq, tq)], "rep", sib
        )
        for i in range(EARLY):
            flight[k, "x", i] = wires.copy(tout.at[k, i], tfar.at[k, i], "rep", across)
        if d:
            flight[k, "late"] = wires.copy(lleave.at[j], lgot.at[j], "node", to_node(d))
            for i in range(EARLY):
                flight[k, "node", i] = wires.copy(
                    leaving.at[j, i], got.at[j, i], "node", to_node(d)
                )
            tail = pl.ds(EARLY, late)
            flight[k, "node", EARLY] = wires.copy(
                leaving.at[j, tail], got.at[j, tail], "node", to_node(d)
            )
    wflight = {
        "x": wires.copy(wout, wfar, "rep", across),
        "over": wires.copy(wfull.at[me], wfull.at[me], "rep", across),
        "side": wires.copy(wfull.at[me], wfull.at[me], "rep", sib),
        "relay": wires.copy(wfull.at[across], wfull.at[across], "rep", sib),
    }
    for i, partner in enumerate(partners):
        wflight[i] = wires.copy(wstep.at[i], wgot.at[i], "node", partner)

    def terms_out(k):
        for q, name in ((diag, "diag"), (sib, "sib"), (across, None), (me, None)):
            for i in range(tq):
                r = q * tq + i
                terms[k, r] = ends(1, k, r).astype(BF16)
            if name:
                flight[k, name].start()

    def terms_cross(k, j, d):
        flight[k, "diag"].wait()
        for i in range(tq):
            value = terms[k, across * tq + i].astype(F32) + tnear[k, i].astype(F32)
            if i < EARLY:
                tout[k, i] = value.astype(BF16)
                flight[k, "x", i].start()
            elif d:
                lleave[j, i - EARLY] = value.astype(BF16)
            else:
                total[tq + i - EARLY] = value
        if d:
            flight[k, "late"].start()
        flight[k, "sib"].wait()
        for i in range(EARLY, tq):
            value = terms[k, me * tq + i].astype(F32) + tnear[k, tq + i].astype(F32)
            if d:
                leaving[j, i] = value.astype(BF16)
            else:
                total[i] = value
        if d:
            flight[k, "node", EARLY].start()

    def terms_leave(k, j, d, i):
        flight[k, "x", i].wait()
        value = terms[k, me * tq + i].astype(F32) + tnear[k, tq + i].astype(F32)
        value = value + tfar[k, i].astype(F32)
        if d:
            leaving[j, i] = value.astype(BF16)
            flight[k, "node", i].start()
        else:
            total[i] = value

    def wgrad_cross():
        for copy in wsib:
            copy.wait()
        wout[...] = (wmine[across].astype(F32) + wnear[0].astype(F32)).astype(BF16)
        wflight["x"].start()

    def wgrad_double(i):
        if i == 0:
            wflight["x"].wait()
            value = wmine[me].astype(F32) + wnear[1].astype(F32) + wfar[...].astype(F32)
        else:
            wflight[i - 1].wait()
            value = wstep[i - 1].astype(F32) + wgot[i - 1].astype(F32)
        if i < len(doubling):
            wstep[i] = value.astype(BF16)
            wflight[i].start()
        else:
            wfull[me] = (value * scale).astype(BF16)
            wflight["over"].start()
            wflight["side"].start()

    def wgrad_relay():
        wflight["over"].wait()
        wflight["relay"].start()

    C = lambda k, j, d: (lambda: terms_cross(k, j, d))
    L = lambda k, j, d, i: (lambda: terms_leave(k, j, d, i))
    W = lambda i: (lambda: wgrad_double(i))
    leg = {0: (0, 0, 1), 2: (2, 1, nodes - 1), 3: (3, 2, nodes - 2), 1: (1, 3, 0)}
    sweep(1, 3, full, [[], [], [wgrad_cross], []])
    terms_out(3)
    sweep(1, 0, full, [[], [C(*leg[3])], [W(0)], []])
    terms_out(0)
    sweep(1, 2, full, [[], [C(*leg[0])], [W(1)], []])
    terms_out(2)
    sweep(1, 1, full, [[L(*leg[3], 0)], [C(*leg[2]), L(*leg[3], 1)], [W(2), L(*leg[3], 2)], []])
    terms_out(1)
    terms_leave(*leg[0], 0)
    terms_cross(*leg[1])
    for i in range(1, EARLY):
        terms_leave(*leg[0], i)
    for i in range(3, len(doubling) + 1):
        wgrad_double(i)
    for i in range(EARLY):
        terms_leave(*leg[2], i)
    spare = [total[tq + i] for i in range(late)]
    for j, k in enumerate((0, 2, 3)):
        flight[k, "late"].wait()
        spare = [spare[i] + lgot[j, i].astype(F32) for i in range(late)]
    for i in range(late):
        lout[i] = spare[i].astype(BF16)
    last_cross = wires.hop(lout, lfar, "rep", across)
    wgrad_relay()
    for i in range(EARLY):
        terms_leave(*leg[1], i)
    wflight["side"].wait()
    wflight["relay"].wait()
    for q in range(4):
        wgrad[q * wrows : (q + 1) * wrows, :] = wfull[q].astype(F32)
    for k in (0, 2, 3):
        for i in range(EARLY + 1):
            flight[k, "node", i].wait()
    last_cross.wait()
    values = []
    for i in range(tq):
        value = total[i]
        for j in range(3):
            value = value + got[j, i].astype(F32)
        if i >= EARLY:
            value = value + lfar[i - EARLY].astype(F32)
        values.append(value.astype(BF16))
    grad[...] = jnp.dot(
        pick[...], jnp.concatenate(values, axis=0), preferred_element_type=F32
    ).astype(grad.dtype)


def fused_call(nodes, scale, counts, row_ids, col_ids, tiles, features, order, cot, weight):
    capacity, size = tiles.shape[1], tiles.shape[-1]
    feat = features.shape[1]
    count = features.shape[0] // size
    tq = count // 4
    late = tq - EARLY
    pairs = (capacity + count) // 2
    steps = nodes.bit_length() - 1
    vmem = pl.BlockSpec(memory_space=pltpu.VMEM)

    def rows(*lead):
        return pltpu.VMEM(lead + (size, feat), BF16)

    def sums(*lead):
        return pltpu.VMEM(lead + (size, feat), F32)

    def wide(*lead):
        return pltpu.VMEM(lead + (feat // 4, feat), BF16)

    flat = pltpu.VMEM((tq * size, feat), BF16)
    return pl.pallas_call(
        functools.partial(fused_kernel, nodes, scale),
        out_shape=(
            jax.ShapeDtypeStruct(cot.shape, BF16),
            jax.ShapeDtypeStruct(cot.shape, BF16),
            jax.ShapeDtypeStruct((feat, feat), F32),
        ),
        in_specs=[pl.BlockSpec(memory_space=pltpu.MemorySpace.HBM)] * 8,
        out_specs=(vmem,) * 3,
        scratch_shapes=[
            pltpu.SMEM(counts.shape, jnp.int32),
            pltpu.VMEM(row_ids.shape, jnp.int32),
            pltpu.VMEM(col_ids.shape, jnp.int32),
            pltpu.VMEM(features.shape, BF16),
            pltpu.VMEM(order.shape, jnp.int32),
            pltpu.VMEM(cot.shape, BF16),
            pltpu.VMEM(weight.shape, BF16),
            pltpu.VMEM((4, capacity + 1, size, size), BF16),
            rows(count), rows(count), rows(count), rows(count),
            sums(pairs + 1), sums(count),
            rows(count), rows(2 * tq), rows(tq), rows(tq), flat, flat, rows(count),
            rows(4, count), rows(4, 2 * tq), rows(4, EARLY), rows(4, EARLY),
            rows(3, tq), rows(3, tq), rows(3, late), rows(3, late),
            sums(tq + late), rows(late), rows(late),
            wide(4), wide(2), wide(), wide(), wide(steps), wide(steps), wide(4),
            pltpu.VMEM((tq * size, tq * size), BF16),
            pltpu.VMEM((128, 128), jnp.int32),
            pltpu.VMEM((8 * FIELDS, 128), jnp.int32),
            pltpu.SMEM((8 * FIELDS, 128), jnp.int32),
            pltpu.SemaphoreType.DMA((5,)),
            pltpu.SemaphoreType.DMA((7,)),
            pltpu.SemaphoreType.DMA((128,)),
            pltpu.SemaphoreType.DMA((128,)),
        ],
        compiler_params=pltpu.CompilerParams(
            collective_id=0, has_side_effects=True, vmem_limit_bytes=VLIM * 1024 * 1024
        ),
    )(counts, row_ids, col_ids, tiles, features, order, cot, weight)


def publish_kernel(*refs):
    n = (len(refs) - 2) // 3
    ins, outs, held = refs[:n], refs[n : 2 * n], refs[2 * n : 3 * n]
    take, give = refs[3 * n], refs[3 * n + 1]
    loads = [pltpu.make_async_copy(ins[i], held[i], take.at[i]) for i in range(n)]
    stores = [pltpu.make_async_copy(held[i], outs[i], give.at[i]) for i in range(n)]
    for load in loads:
        load.start()
    for load, store in zip(loads, stores):
        load.wait()
        store.start()
    for store in stores:
        store.wait()


def publish_call(*arrays):
    n = len(arrays)
    return pl.pallas_call(
        publish_kernel,
        out_shape=tuple(jax.ShapeDtypeStruct(a.shape, a.dtype) for a in arrays),
        in_specs=[pl.BlockSpec(memory_space=pl.ANY)] * n,
        out_specs=(pl.BlockSpec(memory_space=pl.ANY),) * n,
        scratch_shapes=[pltpu.VMEM(a.shape, a.dtype) for a in arrays]
        + [pltpu.SemaphoreType.DMA((n,))] * 2,
        compiler_params=pltpu.CompilerParams(vmem_limit_bytes=VLIM * 1024 * 1024),
    )(*arrays)


def local(features, tiles, tile_rows, tile_cols, tile_count, order, weight, cotangent):
    nodes = lax.axis_size("node")
    size = tiles.shape[-1]
    scale = 1.0 / math.sqrt(features.shape[0] * nodes)
    outs = fused_call(
        nodes, scale, tile_count[0], tile_rows[0, 0], tile_cols[0, 0], tiles[0, 0],
        features, order.reshape(-1, size), cotangent, weight,
    )
    return publish_call(*outs)


def solution(mesh):
    placed = (
        P("node", None),
        P("node", "rep", None, None, None, None),
        P("node", "rep", None, None),
        P("node", "rep", None, None),
        P("node", "rep", None),
        P("node"),
        P(),
        P(("node", "rep"), None),
    )
    return jax.shard_map(
        local,
        mesh=mesh,
        in_specs=placed,
        out_specs=(P(("node", "rep"), None), P(("node", "rep"), None), P()),
        check_vma=False,
    )
```

```python
import functools
import math

import jax
import jax.numpy as jnp
from jax import lax
from jax.experimental import pallas as pl
from jax.experimental.pallas import tpu as pltpu
from jax.sharding import PartitionSpec as P

EXCL = 3
SHARED = 2
EARLY = 2
GROUP = 14
VLIM = 60
FIELDS = 4
F32 = jnp.float32
BF16 = jnp.bfloat16


def sort_slots(capacity, count_ref, rows, cols, out, stage):
    lanes = stage.shape[1]
    zero = jnp.int32(0)
    stage[...] = jnp.zeros_like(stage)
    stage[0:4, 0:capacity] = rows[...]
    stage[4:8, 0:capacity] = cols[...]
    by_slot = stage[...].T
    sub = lax.broadcasted_iota(jnp.int32, (capacity, lanes), 0)
    lane = lax.broadcasted_iota(jnp.int32, (capacity, lanes), 1)
    for way in range(2):
        for k in range(4):
            at, pick = (way * 4 + k) * FIELDS, way * 4 + k
            key = by_slot[0:capacity, pick : pick + 1]
            other = by_slot[0:capacity, (1 - way) * 4 + k : (1 - way) * 4 + k + 1]
            along = stage[pick : pick + 1, :]
            live = sub < count_ref[0, k]
            same = live & (key == along) & (lane < sub)
            rank = jnp.sum(jnp.where(same, 1, zero), axis=1, keepdims=True)
            held = jnp.sum(jnp.where(live & (key == lane), 1, zero), axis=0, keepdims=True)
            odd = held - 2 * lax.shift_right_logical(held, 1)
            padded = held + odd
            base = jnp.sum(jnp.where(lane < key, padded, zero), axis=1, keepdims=True)
            length = jnp.sum(jnp.where(lane == key, padded, zero), axis=1, keepdims=True)
            spot = base + rank
            put = live & (spot == lane)
            slot = jnp.sum(jnp.where(put, sub - capacity, zero), axis=0, keepdims=True)
            source = jnp.sum(jnp.where(put, other, zero), axis=0, keepdims=True)
            starts = jnp.sum(jnp.where(put & (rank == 0), 1, zero), axis=0, keepdims=True)
            reach = jnp.where(live & (key == lane) & (rank == 0), base + length, zero)
            last = lax.shift_right_logical(jnp.sum(reach, axis=0, keepdims=True), 1)
            out[at : at + 1, :] = slot + capacity
            out[at + 1 : at + 2, :] = source
            out[at + 2 : at + 3, :] = 1 - starts
            out[at + 3 : at + 4, :] = last


class Wires:
    def __init__(self, send, recv):
        self.send, self.recv, self.used = send, recv, 0

    def copy(self, src, dst, axis, target):
        at = self.used
        self.used += 1
        return pltpu.make_async_remote_copy(
            src_ref=src,
            dst_ref=dst,
            send_sem=self.send.at[at],
            recv_sem=self.recv.at[at],
            device_id={axis: target},
            device_id_type=pl.DeviceIdType.MESH,
        )

    def hop(self, src, dst, axis, target):
        copy = self.copy(src, dst, axis, target)
        copy.start()
        return copy


def fused_kernel(
    nodes, scale, count_src, row_src, col_src, tiles, feature_src, order_src, cot_src, weight_src,
    act, grad, wgrad, count_ref, row_ids, col_ids, features, order, cot, weight,
    held, here, halo_a, halo_b, halo_c, sums, acc, part, near, outgoing, far, agg, pg, full,
    terms, tnear, tout, tfar, leaving, got, lleave, lgot, total, lout, lfar,
    wmine, wnear, wout, wfar, wstep, wgot, wfull, pick,
    stage, sorted_slots, table, load_sems, stage_sems, send, recv,
):
    capacity = tiles.shape[1]
    count, size, feat = here.shape
    tq = count // 4
    quarter = tq * size
    pairs = (capacity + count) // 2
    me, home = lax.axis_index("rep"), lax.axis_index("node")
    x, c = me // 2, me % 2
    sib, across, diag = x * 2 + 1 - c, (1 - x) * 2 + c, (1 - x) * 2 + 1 - c
    wires = Wires(send, recv)

    def to_node(d):
        return (home + d) % nodes

    doubling = [1 << i for i in range(nodes.bit_length() - 1)]
    partners = []
    for step in doubling:
        low = (home // step) % 2
        partners.append(home + step - 2 * step * low)
    peers = [("rep", sib), ("rep", across)]
    peers += [("node", to_node(d)) for d in (1, nodes - 1, 2, nodes - 2)]
    peers += [("node", p) for p in partners]
    barrier = pltpu.get_barrier_semaphore()
    for axis, target in peers:
        pl.semaphore_signal(
            barrier, inc=1, device_id={axis: target}, device_id_type=pl.DeviceIdType.MESH
        )

    staged = [
        pltpu.make_async_copy(src, dst, stage_sems.at[i])
        for i, (src, dst) in enumerate(
            (
                (order_src, order), (feature_src, features), (count_src, count_ref),
                (row_src, row_ids), (col_src, col_ids), (cot_src, cot), (weight_src, weight),
            )
        )
    ]
    for copy in staged:
        copy.start()
    loads = [
        pltpu.make_async_copy(
            tiles.at[k], held.at[k, pl.ds(0, capacity)], load_sems.at[k]
        )
        for k in (1, 0, 2, 3)
    ]
    for load in loads:
        load.start()

    spots = lax.broadcasted_iota(jnp.int32, (quarter, size), 0)

    def chosen(t):
        return (spots == lax.rem(order[pl.ds(t, 1), :], quarter)).astype(BF16)

    def reorder(t):
        rows = features[pl.ds(pl.multiple_of((t // tq) * quarter, quarter), quarter), :]
        here[t] = lax.dot_general(
            chosen(t), rows, (((0,), (0,)), ((), ())), preferred_element_type=F32
        ).astype(BF16)

    first = 10 * x + EXCL * c
    common = 2 * 2 * EXCL // 2 + SHARED * c
    other = 10 * (1 - x) + EXCL * c
    for copy in staged[:2]:
        copy.wait()
    for i in range(EXCL):
        reorder(first + i)
    for i in range(SHARED):
        reorder(common + i)
    pl.semaphore_wait(barrier, len(peers))

    moves = ((2, halo_a), (nodes - 1, halo_b), (1, halo_c))
    direct, shared = [], []
    for d, land in moves:
        direct.append(
            [
                wires.hop(here.at[first + i], land.at[first + i], "node", to_node(d))
                for i in range(EXCL)
            ]
        )
        block = pl.ds(common, SHARED)
        shared.append(wires.hop(here.at[block], land.at[block], "node", to_node(d)))
    for i in range(EXCL):
        reorder(other + i)
    rest = 10 * x + EXCL * (1 - c)
    for i in range(EXCL):
        reorder(rest + i)
        reorder(10 * (1 - x) + EXCL * (1 - c) + i)
    for i in range(SHARED):
        reorder(2 * EXCL + SHARED * (1 - c) + i)
    for copy in staged[2:]:
        copy.wait()
    sort_slots(capacity, count_ref, row_ids, col_ids, sorted_slots, stage)
    fetch = pltpu.make_async_copy(sorted_slots, table, load_sems.at[4])
    fetch.start()
    for k in range(4):
        held[k, capacity] = jnp.zeros((size, size), BF16)
    sums[0] = jnp.zeros((size, feat), F32)
    mine_pick = jnp.concatenate([chosen(me * tq + i) for i in range(tq)], axis=1)
    pick[...] = mine_pick

    crossing, aside_direct, aside_cross, aside_shared = [], [], [], []
    for d, land in moves:
        for i in range(EXCL):
            near_tile, far_tile = land.at[first + i], land.at[other + i]
            crossing.append(wires.copy(near_tile, near_tile, "rep", across))
            aside_direct.append(wires.copy(near_tile, near_tile, "rep", sib))
            aside_cross.append(wires.copy(far_tile, far_tile, "rep", sib))
        both = land.at[pl.ds(common, SHARED)]
        aside_shared.append(wires.copy(both, both, "rep", sib))

    def event_direct(g):
        direct[g // EXCL][g % EXCL].wait()
        crossing[g].start()
        aside_direct[g].start()

    def event_cross(g):
        crossing[g].wait()
        aside_cross[g].start()

    def event_shared(j):
        shared[j].wait()
        aside_shared[j].start()

    def settle(j):
        for i in range(EXCL):
            aside_direct[j * EXCL + i].wait()
            aside_cross[j * EXCL + i].wait()
        aside_shared[j].wait()

    def product(way, k, i, source):
        at = (way * 4 + k) * FIELDS
        one, two = held[k, table[at, 2 * i]], held[k, table[at, 2 * i + 1]]
        left, right = source[table[at + 1, 2 * i]], source[table[at + 1, 2 * i + 1]]
        rows = jnp.concatenate([left, right], axis=0)
        if way == 0:
            return jnp.dot(
                jnp.concatenate([one, two], axis=1), rows, preferred_element_type=F32
            )
        return lax.dot_general(
            jnp.concatenate([one, two], axis=0), rows, (((0,), (0,)), ((), ())),
            preferred_element_type=F32,
        )

    def sweep(way, k, source, events):
        at = (way * 4 + k) * FIELDS

        def body(step, _):
            for turn, work in enumerate(events):
                if work:
                    @pl.when(step == turn)
                    def _(work=work):
                        for f in work:
                            f()
            base = step * GROUP
            products = [product(way, k, base + g, source) for g in range(GROUP)]
            value = sums[base]
            for g in range(GROUP):
                value = products[g] + table[at + 2, 2 * (base + g)].astype(F32) * value
                sums[base + g + 1] = value
            return 0

        lax.fori_loop(0, pairs // GROUP, body, 0)

    def ends(way, k, r):
        return sums[table[(way * 4 + k) * FIELDS + 3, r]]

    def run(*work):
        for f in work:
            f()

    E = lambda g: (lambda: event_direct(g))
    X = lambda g: (lambda: event_cross(g))
    S = lambda j: (lambda: event_shared(j))

    fetch.wait()
    for load in loads:
        load.wait()
    sweep(0, 1, here, [[E(0)], [E(1)], [E(2), X(0)], [E(3), X(1)]])
    for r in range(count):
        acc[r] = ends(0, 1, r)
    run(E(4), X(2), S(0))
    settle(0)
    sweep(0, 3, halo_a, [[E(5), X(3)], [E(6), X(4)], [E(7), X(5)], [E(8), X(6)]])
    for r in range(count):
        acc[r] += ends(0, 3, r)
    run(S(1))
    settle(1)
    sweep(0, 0, halo_b, [[X(7)], [X(8), S(2)], [], []])
    for r in range(count):
        acc[r] += ends(0, 0, r)
    settle(2)
    sweep(0, 2, halo_c, [[], [], [], []])

    def finish_rows(q):
        for i in range(tq):
            r = q * tq + i
            value = acc[r] + ends(0, 2, r)
            acc[r] = value
            part[r] = value.astype(BF16)

    finish_rows(diag)
    to_sib = [
        wires.hop(part.at[diag * tq + i], near.at[i], "rep", sib) for i in range(tq)
    ]
    finish_rows(sib)
    block = pl.ds(sib * tq, tq)
    rest_sib = wires.hop(part.at[block], near.at[pl.ds(tq, tq)], "rep", sib)
    finish_rows(across)
    crossed = []
    for i in range(tq):
        to_sib[i].wait()
        outgoing[i] = (acc[across * tq + i] + near[i].astype(F32)).astype(BF16)
        crossed.append(wires.hop(outgoing.at[i], far.at[i], "rep", across))
    finish_rows(me)
    rest_sib.wait()
    over, side, relay = [], [], []
    for i in range(tq):
        r = me * tq + i
        mine = acc[r] + near[tq + i].astype(F32)
        crossed[i].wait()
        aggregate = (mine + far[i].astype(F32)).astype(BF16)
        agg[i * size : (i + 1) * size, :] = aggregate
        pre_act = jnp.dot(aggregate, weight[...], preferred_element_type=F32)
        gate = jax.nn.sigmoid(pre_act)
        act[i * size : (i + 1) * size, :] = (pre_act * gate).astype(act.dtype)
        pre_grad = (
            cot[i * size : (i + 1) * size, :].astype(F32) * gate * (1.0 + pre_act * (1.0 - gate))
        ).astype(BF16)
        pg[i * size : (i + 1) * size, :] = pre_grad
        full[r] = lax.dot_general(
            pre_grad, weight[...], (((1,), (1,)), ((), ())), preferred_element_type=F32
        ).astype(BF16)
        over.append(wires.hop(full.at[r], full.at[r], "rep", across))
        side.append(wires.hop(full.at[r], full.at[r], "rep", sib))
    wrows = feat // 4
    wpart = lax.dot_general(
        agg[...], pg[...], (((0,), (0,)), ((), ())), preferred_element_type=F32
    )
    for q in range(4):
        wmine[q] = wpart[q * wrows : (q + 1) * wrows, :].astype(BF16)
    for i in range(tq):
        over[i].wait()
        r = across * tq + i
        relay.append(wires.hop(full.at[r], full.at[r], "rep", sib))
    wsib = [
        wires.hop(wmine.at[diag], wnear.at[0], "rep", sib),
        wires.hop(wmine.at[sib], wnear.at[1], "rep", sib),
    ]
    for copy in side + relay:
        copy.wait()

    late = tq - EARLY
    flight = {}
    for k, j, d in ((0, 0, 1), (2, 1, nodes - 1), (3, 2, nodes - 2), (1, 3, 0)):
        flight[k, "diag"] = wires.copy(
            terms.at[k, pl.ds(diag * tq, tq)], tnear.at[k, pl.ds(0, tq)], "rep", sib
        )
        flight[k, "sib"] = wires.copy(
            terms.at[k, pl.ds(sib * tq, tq)], tnear.at[k, pl.ds(tq, tq)], "rep", sib
        )
        for i in range(EARLY):
            flight[k, "x", i] = wires.copy(tout.at[k, i], tfar.at[k, i], "rep", across)
        if d:
            flight[k, "late"] = wires.copy(lleave.at[j], lgot.at[j], "node", to_node(d))
            for i in range(EARLY):
                flight[k, "node", i] = wires.copy(
                    leaving.at[j, i], got.at[j, i], "node", to_node(d)
                )
            tail = pl.ds(EARLY, late)
            flight[k, "node", EARLY] = wires.copy(
                leaving.at[j, tail], got.at[j, tail], "node", to_node(d)
            )
    wflight = {
        "x": wires.copy(wout, wfar, "rep", across),
        "over": wires.copy(wfull.at[me], wfull.at[me], "rep", across),
        "side": wires.copy(wfull.at[me], wfull.at[me], "rep", sib),
        "relay": wires.copy(wfull.at[across], wfull.at[across], "rep", sib),
    }
    for i, partner in enumerate(partners):
        wflight[i] = wires.copy(wstep.at[i], wgot.at[i], "node", partner)

    def terms_out(k):
        for q, name in ((diag, "diag"), (sib, "sib"), (across, None), (me, None)):
            for i in range(tq):
                r = q * tq + i
                terms[k, r] = ends(1, k, r).astype(BF16)
            if name:
                flight[k, name].start()

    def terms_cross(k, j, d):
        flight[k, "diag"].wait()
        for i in range(tq):
            value = terms[k, across * tq + i].astype(F32) + tnear[k, i].astype(F32)
            if i < EARLY:
                tout[k, i] = value.astype(BF16)
                flight[k, "x", i].start()
            elif d:
                lleave[j, i - EARLY] = value.astype(BF16)
            else:
                total[tq + i - EARLY] = value
        if d:
            flight[k, "late"].start()
        flight[k, "sib"].wait()
        for i in range(EARLY, tq):
            value = terms[k, me * tq + i].astype(F32) + tnear[k, tq + i].astype(F32)
            if d:
                leaving[j, i] = value.astype(BF16)
            else:
                total[i] = value
        if d:
            flight[k, "node", EARLY].start()

    def terms_leave(k, j, d, i):
        flight[k, "x", i].wait()
        value = terms[k, me * tq + i].astype(F32) + tnear[k, tq + i].astype(F32)
        value = value + tfar[k, i].astype(F32)
        if d:
            leaving[j, i] = value.astype(BF16)
            flight[k, "node", i].start()
        else:
            total[i] = value

    def wgrad_cross():
        for copy in wsib:
            copy.wait()
        wout[...] = (wmine[across].astype(F32) + wnear[0].astype(F32)).astype(BF16)
        wflight["x"].start()

    def wgrad_double(i):
        if i == 0:
            wflight["x"].wait()
            value = wmine[me].astype(F32) + wnear[1].astype(F32) + wfar[...].astype(F32)
        else:
            wflight[i - 1].wait()
            value = wstep[i - 1].astype(F32) + wgot[i - 1].astype(F32)
        if i < len(doubling):
            wstep[i] = value.astype(BF16)
            wflight[i].start()
        else:
            wfull[me] = (value * scale).astype(BF16)
            wflight["over"].start()
            wflight["side"].start()

    def wgrad_relay():
        wflight["over"].wait()
        wflight["relay"].start()

    C = lambda k, j, d: (lambda: terms_cross(k, j, d))
    L = lambda k, j, d, i: (lambda: terms_leave(k, j, d, i))
    W = lambda i: (lambda: wgrad_double(i))
    leg = {0: (0, 0, 1), 2: (2, 1, nodes - 1), 3: (3, 2, nodes - 2), 1: (1, 3, 0)}
    sweep(1, 3, full, [[], [], [wgrad_cross], []])
    terms_out(3)
    sweep(1, 0, full, [[], [C(*leg[3])], [W(0)], []])
    terms_out(0)
    sweep(1, 2, full, [[], [C(*leg[0])], [W(1)], []])
    terms_out(2)
    sweep(1, 1, full, [[L(*leg[3], 0)], [C(*leg[2]), L(*leg[3], 1)], [W(2)], []])
    terms_out(1)
    terms_leave(*leg[0], 0)
    terms_cross(*leg[1])
    for i in range(1, EARLY):
        terms_leave(*leg[0], i)
    for i in range(3, len(doubling) + 1):
        wgrad_double(i)
    for i in range(EARLY):
        terms_leave(*leg[2], i)
    spare = [total[tq + i] for i in range(late)]
    for j, k in enumerate((0, 2, 3)):
        flight[k, "late"].wait()
        spare = [spare[i] + lgot[j, i].astype(F32) for i in range(late)]
    for i in range(late):
        lout[i] = spare[i].astype(BF16)
    last_cross = wires.hop(lout, lfar, "rep", across)
    wgrad_relay()
    for i in range(EARLY):
        terms_leave(*leg[1], i)
    wflight["side"].wait()
    wflight["relay"].wait()
    for q in range(4):
        wgrad[q * wrows : (q + 1) * wrows, :] = wfull[q].astype(F32)
    for k in (0, 2, 3):
        for i in range(EARLY + 1):
            flight[k, "node", i].wait()
    last_cross.wait()
    values = []
    for i in range(tq):
        value = total[i]
        for j in range(3):
            value = value + got[j, i].astype(F32)
        if i >= EARLY:
            value = value + lfar[i - EARLY].astype(F32)
        values.append(value.astype(BF16))
    grad[...] = jnp.dot(
        pick[...], jnp.concatenate(values, axis=0), preferred_element_type=F32
    ).astype(grad.dtype)


def fused_call(nodes, scale, counts, row_ids, col_ids, tiles, features, order, cot, weight):
    capacity, size = tiles.shape[1], tiles.shape[-1]
    feat = features.shape[1]
    count = features.shape[0] // size
    tq = count // 4
    late = tq - EARLY
    pairs = (capacity + count) // 2
    steps = nodes.bit_length() - 1
    vmem = pl.BlockSpec(memory_space=pltpu.VMEM)

    def rows(*lead):
        return pltpu.VMEM(lead + (size, feat), BF16)

    def sums(*lead):
        return pltpu.VMEM(lead + (size, feat), F32)

    def wide(*lead):
        return pltpu.VMEM(lead + (feat // 4, feat), BF16)

    flat = pltpu.VMEM((tq * size, feat), BF16)
    return pl.pallas_call(
        functools.partial(fused_kernel, nodes, scale),
        out_shape=(
            jax.ShapeDtypeStruct(cot.shape, BF16),
            jax.ShapeDtypeStruct(cot.shape, BF16),
            jax.ShapeDtypeStruct((feat, feat), F32),
        ),
        in_specs=[pl.BlockSpec(memory_space=pltpu.MemorySpace.HBM)] * 8,
        out_specs=(vmem,) * 3,
        scratch_shapes=[
            pltpu.SMEM(counts.shape, jnp.int32),
            pltpu.VMEM(row_ids.shape, jnp.int32),
            pltpu.VMEM(col_ids.shape, jnp.int32),
            pltpu.VMEM(features.shape, BF16),
            pltpu.VMEM(order.shape, jnp.int32),
            pltpu.VMEM(cot.shape, BF16),
            pltpu.VMEM(weight.shape, BF16),
            pltpu.VMEM((4, capacity + 1, size, size), BF16),
            rows(count), rows(count), rows(count), rows(count),
            sums(pairs + 1), sums(count),
            rows(count), rows(2 * tq), rows(tq), rows(tq), flat, flat, rows(count),
            rows(4, count), rows(4, 2 * tq), rows(4, EARLY), rows(4, EARLY),
            rows(3, tq), rows(3, tq), rows(3, late), rows(3, late),
            sums(tq + late), rows(late), rows(late),
            wide(4), wide(2), wide(), wide(), wide(steps), wide(steps), wide(4),
            pltpu.VMEM((tq * size, tq * size), BF16),
            pltpu.VMEM((128, 128), jnp.int32),
            pltpu.VMEM((8 * FIELDS, 128), jnp.int32),
            pltpu.SMEM((8 * FIELDS, 128), jnp.int32),
            pltpu.SemaphoreType.DMA((5,)),
            pltpu.SemaphoreType.DMA((7,)),
            pltpu.SemaphoreType.DMA((128,)),
            pltpu.SemaphoreType.DMA((128,)),
        ],
        compiler_params=pltpu.CompilerParams(
            collective_id=0, has_side_effects=True, vmem_limit_bytes=VLIM * 1024 * 1024
        ),
    )(counts, row_ids, col_ids, tiles, features, order, cot, weight)


def publish_kernel(*refs):
    n = (len(refs) - 2) // 3
    ins, outs, held = refs[:n], refs[n : 2 * n], refs[2 * n : 3 * n]
    take, give = refs[3 * n], refs[3 * n + 1]
    loads = [pltpu.make_async_copy(ins[i], held[i], take.at[i]) for i in range(n)]
    stores = [pltpu.make_async_copy(held[i], outs[i], give.at[i]) for i in range(n)]
    for load in loads:
        load.start()
    for load, store in zip(loads, stores):
        load.wait()
        store.start()
    for store in stores:
        store.wait()


def publish_call(*arrays):
    n = len(arrays)
    return pl.pallas_call(
        publish_kernel,
        out_shape=tuple(jax.ShapeDtypeStruct(a.shape, a.dtype) for a in arrays),
        in_specs=[pl.BlockSpec(memory_space=pl.ANY)] * n,
        out_specs=(pl.BlockSpec(memory_space=pl.ANY),) * n,
        scratch_shapes=[pltpu.VMEM(a.shape, a.dtype) for a in arrays]
        + [pltpu.SemaphoreType.DMA((n,))] * 2,
        compiler_params=pltpu.CompilerParams(vmem_limit_bytes=VLIM * 1024 * 1024),
    )(*arrays)


def local(features, tiles, tile_rows, tile_cols, tile_count, order, weight, cotangent):
    nodes = lax.axis_size("node")
    size = tiles.shape[-1]
    scale = 1.0 / math.sqrt(features.shape[0] * nodes)
    outs = fused_call(
        nodes, scale, tile_count[0], tile_rows[0, 0], tile_cols[0, 0], tiles[0, 0],
        features, order.reshape(-1, size), cotangent, weight,
    )
    return publish_call(*outs)


def solution(mesh):
    placed = (
        P("node", None),
        P("node", "rep", None, None, None, None),
        P("node", "rep", None, None),
        P("node", "rep", None, None),
        P("node", "rep", None),
        P("node"),
        P(),
        P(("node", "rep"), None),
    )
    return jax.shard_map(
        local,
        mesh=mesh,
        in_specs=placed,
        out_specs=(P(("node", "rep"), None), P(("node", "rep"), None), P()),
        check_vma=False,
    )
```
